512 devices in a mesh: section: 8 (over y), dp: 16 (over z, core), tensor: 4 (over x).
Axes of the slice: x: 4, y: 8, z: 8, core: 2. Of those that a mesh axis runs over, the one named last changes fastest.
Arguments:
- section_inputs: bfloat16 [8, 128, 2560], P('section', 'dp', 'tensor'), may hold values from -40 to 40
- entering: bfloat16 [1, 128, 2560], P(None, 'dp', 'tensor'), may hold values from -40 to 40
- grad_outputs: bfloat16 [8, 128, 2560], P('section', 'dp', 'tensor'), may hold values from -6 to 6
- arriving: bfloat16 [1, 128, 2560], P(None, 'dp', 'tensor'), may hold values from -6 to 6
- live_rows: int32 [1], replicated, may hold values from 64 to 128
- stashed_inputs: bfloat16 [8, 2, 128, 2560], P('section', None, 'dp', 'tensor'), may hold values from -40 to 40
- norm_gain: bfloat16 [8, 2560], P('section', 'tensor'), may hold values from 0.25 to 1.75
- up_weight: bfloat16 [8, 2560, 14336], P('section', 'tensor', 'dp'), may hold values from -0.125 to 0.125
- down_weight: bfloat16 [8, 14336, 2560], P('section', 'dp', 'tensor'), may hold values from -0.046875 to 0.046875
- held_blocks: int32 [8, 4, 16, 6], P('section', 'tensor'), may hold values from 0 to 69, as said below
- held_count: int32 [8, 4, 16], P('section', 'tensor'), may hold values from 1 to 6, as said below
- held_owner: int32 [8, 4, 16, 6], P('section', 'tensor'), may hold values from 0 to 15, as said below
- first_moment: float32 [8, 4, 16, 6, 128, 128], P('section', 'tensor', 'dp'), may hold values from -4 to 4
- second_moment: float32 [8, 4, 16, 6, 128, 128], P('section', 'tensor', 'dp'), may hold values from 0.01 to 1
Outputs:
- section_outputs: bfloat16 [8, 2, 128, 2560], P('section', None, 'dp', 'tensor')
- input_grads: bfloat16 [8, 2, 128, 2560], P('section', None, 'dp', 'tensor')
- first_next: float32 [8, 4, 16, 6, 128, 128], P('section', 'tensor', 'dp')
- second_next: float32 [8, 4, 16, 6, 128, 128], P('section', 'tensor', 'dp')
- update_direction: float32 [8, 4, 16, 6, 128, 128], P('section', 'tensor', 'dp')
The draws below stay inside these ranges and needn't reach their ends.
Inputs may be any that keep to these rules, and one draw needn't show every extreme that they name: `held_blocks`: A number below 35 names a block of the device's up projection share, row-major over 5 x 7 blocks; the others, less 35, a block of its down projection share, row-major over 7 x 5 blocks. A device's first held_count entries are distinct; later entries are not used. `held_count`: some device of each section and tensor index lists 6 trainable blocks. `held_owner`: the owners of one device's trainable blocks are distinct and never the device itself. Each dp index owns at most 6 blocks of one section and tensor index, and some owns exactly 6.
All inputs are finite; a program needn't handle non-finite values.
Results may differ from the reference program's by a relative error of at most 0.015.
Values may be sent and summed in bfloat16 or wider, within the bound.
A program may use at most 64 MiB of HBM per device.

```python
import math
import jax
import jax.numpy as jnp
from jax import lax

DW = 2560
FF = 14336
BLK = 128
TURNS = 2
ROWS = 128
HCAP = 6
N_SECTION = 8
N_DP = 16
N_TENSOR = 4


def spread_rows(key, leading):
    key_base, key_rows, key_cols = jax.random.split(key, 3)
    full_shape = leading + (ROWS, DW)
    samples = jnp.clip(jax.random.normal(key_base, full_shape, jnp.float32), -4.0, 4.0)
    row_scales = jnp.power(10.0, jax.random.uniform(key_rows, leading + (ROWS, 1), jnp.float32, -0.5, 0.5))
    col_scales = jnp.power(10.0, jax.random.uniform(key_cols, leading + (1, DW), jnp.float32, -0.5, 0.5))
    return (samples * row_scales * col_scales).astype(jnp.bfloat16)


def draw_section_inputs(key, part):
    return spread_rows(key, (N_SECTION,))


def draw_entering(key, part):
    return spread_rows(key, (TURNS - 1,))


def draw_stashed_inputs(key, part):
    return spread_rows(key, (N_SECTION, TURNS))


def ownership(key):
    capacity = HCAP
    light_top = max(2, capacity // 2)

    def column(column_key):
        key_order, key_light, key_turn = jax.random.split(column_key, 3)
        cyclic_order = jax.random.permutation(key_order, N_DP).astype(jnp.int32)
        position = jnp.argsort(cyclic_order).astype(jnp.int32)
        light_counts = jax.random.randint(key_light, (N_DP,), 1, light_top + 1)
        counts_by_position = jnp.where(jnp.arange(N_DP) < capacity, capacity, light_counts)
        counts = counts_by_position[position]
        rotation = jax.random.randint(key_turn, (N_DP,), 0, capacity)
        slot_ids = jnp.arange(capacity)
        offsets = (slot_ids[None, :] + rotation[:, None]) % capacity + 1
        owners = cyclic_order[(position[:, None] + offsets) % N_DP]
        return (counts.astype(jnp.int32), owners.astype(jnp.int32))
    key_list = jax.random.split(jax.random.fold_in(key, 11), N_SECTION * N_TENSOR)
    counts, owners = jax.vmap(column)(key_list)
    return (counts.reshape(N_SECTION, N_TENSOR, N_DP), owners.reshape(N_SECTION, N_TENSOR, N_DP, HCAP))


def draw_held_count(key, part):
    return ownership(key)[0]


def draw_held_owner(key, part):
    return ownership(key)[1]


def draw_held_blocks(key, part):
    block_total = 2 * (DW // (N_TENSOR * BLK)) * (FF // (N_DP * BLK))
    key_list = jax.random.split(jax.random.fold_in(key, 5), N_SECTION * N_TENSOR * N_DP)
    chosen_ids = jax.vmap(lambda one_key: jax.random.permutation(one_key, block_total)[:HCAP])(key_list)
    return chosen_ids.reshape(N_SECTION, N_TENSOR, N_DP, HCAP).astype(jnp.int32)


def block_scale(rng, shape, shards, smallest, high):
    loudness = 1.0
    for dim, parts in shards:
        heights = jax.random.uniform(jax.random.fold_in(jax.random.fold_in(rng, 6), dim), (parts,), jnp.float32, smallest / len(shards), high / len(shards))
        loudness = loudness * jnp.repeat(jnp.exp(heights), shape[dim] // parts).reshape((-1,) + (1,) * (len(shape) - 1 - dim))
    return loudness


def gaussian(key, dims, deviation, bound, pieces=(), kind=jnp.bfloat16):
    values = jax.random.normal(key, dims, jnp.float32) * deviation
    if len(pieces) > 0:
        values = block_scale(key, dims, pieces, -0.22, 0.18) * values
    return jnp.clip(values, min=-bound, max=bound).astype(kind)


def setup_inputs(seed: int = 0) -> dict:
    seeds = jax.random.split(jax.random.key(seed), 15)
    return {
        "section_inputs": draw_section_inputs(jax.random.fold_in(seeds[14], 71), 0),
        "entering": draw_entering(jax.random.fold_in(seeds[14], 71), 0),
        "grad_outputs": gaussian(seeds[2], (N_SECTION, ROWS, DW), 1.0, 6.0, ((0, 8), (1, 16), (2, 4))),
        "arriving": gaussian(seeds[3], (TURNS - 1, ROWS, DW), 1.0, 6.0, ((1, 16), (2, 4))),
        "live_rows": jax.random.randint(seeds[4], (TURNS - 1,), ROWS // 2, ROWS + 1).astype(jnp.int32),
        "stashed_inputs": draw_stashed_inputs(jax.random.fold_in(seeds[14], 71), 0),
        "norm_gain": jnp.clip(1.0 + 0.15 * jax.random.normal(seeds[6], (N_SECTION, DW), jnp.float32), 0.25, 1.75).astype(jnp.bfloat16),
        "up_weight": gaussian(seeds[7], (N_SECTION, DW, FF), DW ** -0.5, 0.125, ((0, 8), (1, 4), (2, 16))),
        "down_weight": gaussian(seeds[8], (N_SECTION, FF, DW), FF ** -0.5, 0.046875, ((0, 8), (1, 16), (2, 4))),
        "held_blocks": draw_held_blocks(jax.random.fold_in(seeds[14], 71), 0),
        "held_count": draw_held_count(jax.random.fold_in(seeds[14], 71), 0),
        "held_owner": draw_held_owner(jax.random.fold_in(seeds[14], 71), 0),
        "first_moment": gaussian(seeds[12], (N_SECTION, N_TENSOR, N_DP, HCAP, BLK, BLK), 1.0, 4.0, ((0, 8), (1, 4), (2, 16)), jnp.float32),
        "second_moment": jnp.clip(jnp.exp(math.log(1.0) - 4.6051702 * jax.random.uniform(seeds[13], (N_SECTION, N_TENSOR, N_DP, HCAP, BLK, BLK), jnp.float32) ** block_scale(seeds[13], (N_SECTION, N_TENSOR, N_DP, HCAP, BLK, BLK), ((0, 8), (1, 4), (2, 16)), -0.2, 0.2)), 0.01, 1.0),
    }


EPSILON = 1e-06

def normed_product(rows_in, gain_row, up_matrix):
    widened = rows_in.astype(jnp.float32)
    squares = lax.optimization_barrier(jnp.sum(widened * widened, axis=1))
    normed = (widened * gain_row.astype(jnp.float32)).astype(jnp.bfloat16)
    product = jnp.dot(normed, up_matrix, preferred_element_type=jnp.float32)
    row_scales = lax.rsqrt(squares / DW + EPSILON)
    return (normed, product, row_scales)

def layer_forward(rows_in, gain_row, up_matrix, down_matrix):
    normed, product, row_scales = normed_product(rows_in, gain_row, up_matrix)
    hidden = product * row_scales[:, None]
    activated = (hidden * jax.nn.sigmoid(hidden)).astype(jnp.bfloat16)
    mixed_rows = jnp.dot(activated, down_matrix, preferred_element_type=jnp.float32)
    return (rows_in.astype(jnp.float32) + mixed_rows).astype(jnp.bfloat16)

def block_gradients(normed, activated, scaled_grad, grads_in, held_list):
    channel_total = DW // BLK
    hidden_total = FF // BLK
    channel_blocks = DW // (N_TENSOR * BLK)
    hidden_blocks = FF // (N_DP * BLK)
    up_count = channel_blocks * hidden_blocks
    left_table = jnp.concatenate([normed.reshape(ROWS, channel_total, BLK), activated.reshape(ROWS, hidden_total, BLK)], axis=1)
    right_table = jnp.concatenate([scaled_grad.reshape(ROWS, hidden_total, BLK), grads_in.reshape(ROWS, channel_total, BLK)], axis=1)
    tensor_ids = jnp.arange(N_TENSOR, dtype=jnp.int32)[:, None, None]
    holder_ids = jnp.arange(N_DP, dtype=jnp.int32)[None, :, None]
    down_number = held_list - up_count
    is_up = held_list < up_count
    left_index = jnp.where(is_up, tensor_ids * channel_blocks + held_list // hidden_blocks, channel_total + holder_ids * hidden_blocks + down_number // channel_blocks)
    right_index = jnp.where(is_up, holder_ids * hidden_blocks + held_list % hidden_blocks, hidden_total + tensor_ids * channel_blocks + down_number % channel_blocks)
    left_pick = jnp.take(left_table, left_index.reshape(-1).astype(jnp.int32), axis=1).astype(jnp.float32)
    right_pick = jnp.take(right_table, right_index.reshape(-1).astype(jnp.int32), axis=1).astype(jnp.float32)
    block_grads = jnp.einsum('rkb,rkc->kbc', left_pick, right_pick)
    return block_grads.reshape(N_TENSOR, N_DP, HCAP, BLK, BLK)

def layer_backward(rows_in, grads_in, gain_row, up_matrix, down_matrix, held_list):
    normed, product, row_scales = normed_product(rows_in, gain_row, up_matrix)
    hidden = product * row_scales[:, None]
    sigmoid_part = jax.nn.sigmoid(hidden)
    activated = (hidden * sigmoid_part).astype(jnp.bfloat16)
    act_grad = jnp.dot(grads_in, down_matrix.T, preferred_element_type=jnp.float32)
    hidden_grad = act_grad * sigmoid_part * (1.0 + hidden * (1.0 - sigmoid_part))
    scaled_grad = (hidden_grad * row_scales[:, None]).astype(jnp.bfloat16)
    scale_grad = lax.optimization_barrier(jnp.sum(hidden_grad * product, axis=1))
    normed_grad = jnp.dot(scaled_grad, up_matrix.T, preferred_element_type=jnp.float32)
    widened = rows_in.astype(jnp.float32)
    input_grad = grads_in.astype(jnp.float32) + normed_grad * gain_row.astype(jnp.float32) - (scale_grad * row_scales ** 3)[:, None] * widened / DW
    block_grads = block_gradients(normed, activated, scaled_grad, grads_in, held_list)
    return (input_grad.astype(jnp.bfloat16), block_grads)

def route_blocks(block_grads, counts, owners):
    slot_ids = jnp.arange(HCAP, dtype=jnp.int32)
    dp_ids = jnp.arange(N_DP, dtype=jnp.int32)
    live_slots = slot_ids[None, None, :] < counts[:, :, None]
    chosen = (owners[:, :, None, :] == dp_ids[None, None, :, None]) & live_slots[:, :, None, :]
    is_sent = jnp.any(chosen, axis=3)
    slot_pick = lax.optimization_barrier(jnp.sum(jnp.where(chosen, slot_ids, 0), axis=3)).astype(jnp.int32)
    sent_grads = jnp.take_along_axis(block_grads, slot_pick[:, :, :, None, None], axis=2)
    sent_grads = jnp.where(is_sent[..., None, None], sent_grads, 0.0)
    sent_count = is_sent.astype(jnp.int32)
    ranks = jnp.cumsum(sent_count, axis=1) - sent_count
    matches = is_sent[:, :, :, None] & (ranks[:, :, :, None] == slot_ids)
    is_filled = jnp.any(matches, axis=1)
    source_ids = lax.optimization_barrier(jnp.sum(jnp.where(matches, dp_ids[None, :, None, None], 0), axis=1)).astype(jnp.int32)
    by_owner = jnp.swapaxes(sent_grads, 1, 2)
    owned_grads = jnp.take_along_axis(by_owner, source_ids[..., None, None], axis=2)
    owned_grads = jnp.where(is_filled[..., None, None], owned_grads, 0.0)
    return (owned_grads, is_filled)

def reference(section_inputs, entering, grad_outputs, arriving, live_rows, stashed_inputs, norm_gain, up_weight, down_weight, held_blocks, held_count, held_owner, first_moment, second_moment):
    forward_table = [[None] * TURNS for layer_index in range(N_SECTION)]
    for turn in range(TURNS):
        for layer_index in range(N_SECTION):
            if turn == 0:
                rows_in = section_inputs[layer_index]
            elif layer_index == 0:
                rows_in = entering[turn - 1]
            else:
                rows_in = forward_table[layer_index - 1][turn - 1]
            forward_table[layer_index][turn] = layer_forward(rows_in, norm_gain[layer_index], up_weight[layer_index], down_weight[layer_index])
    row_ids = jnp.arange(ROWS, dtype=jnp.int32)
    backward_table = [[None] * TURNS for layer_index in range(N_SECTION)]
    grad_sums = [jnp.zeros((N_TENSOR, N_DP, HCAP, BLK, BLK), jnp.float32) for layer_index in range(N_SECTION)]
    for turn in range(TURNS):
        for layer_index in range(N_SECTION):
            if turn == 0:
                grads_in = grad_outputs[layer_index]
            elif layer_index == N_SECTION - 1:
                grads_in = jnp.where((row_ids < live_rows[turn - 1])[:, None], arriving[turn - 1], jnp.zeros_like(arriving[turn - 1]))
            else:
                grads_in = backward_table[layer_index + 1][turn - 1]
            result, block_grads = layer_backward(stashed_inputs[layer_index, turn], grads_in, norm_gain[layer_index], up_weight[layer_index], down_weight[layer_index], held_blocks[layer_index])
            backward_table[layer_index][turn] = result
            grad_sums[layer_index] = grad_sums[layer_index] + block_grads
    first_list = []
    second_list = []
    direction_list = []
    for layer_index in range(N_SECTION):
        owned_grads, is_filled = route_blocks(grad_sums[layer_index], held_count[layer_index], held_owner[layer_index])
        filled = is_filled[..., None, None]
        first_new = 0.9 * first_moment[layer_index] + 0.1 * owned_grads
        second_new = 0.999 * second_moment[layer_index] + 0.001 * owned_grads * owned_grads
        direction = first_new / (jnp.sqrt(second_new) + 1e-08)
        first_list.append(jnp.where(filled, first_new, 0.0))
        second_list.append(jnp.where(filled, second_new, 0.0))
        direction_list.append(jnp.where(filled, direction, 0.0))
    section_outputs = jnp.stack([jnp.stack(forward_table[layer_index]) for layer_index in range(N_SECTION)])
    input_grads = jnp.stack([jnp.stack(backward_table[layer_index]) for layer_index in range(N_SECTION)])
    return (section_outputs, input_grads, jnp.stack(first_list), jnp.stack(second_list), jnp.stack(direction_list))
```

```python
import functools

import jax
import jax.numpy as jnp
from jax import lax
from jax.experimental import pallas as pl
from jax.experimental.pallas import tpu as pltpu
from jax.sharding import PartitionSpec as P

MESH = pl.DeviceIdType.MESH
BLK = 128
LANES = 128
EPSILON = 1e-06
F32 = jnp.float32
BF16 = jnp.bfloat16


def times_transposed(left, right):
    return lax.dot_general(left, right, (((1,), (1,)), ((), ())), preferred_element_type=F32)


def lane_blocks_sum(value):
    total = value[:, :LANES]
    for start in range(LANES, value.shape[1], LANES):
        total = total + value[:, start : start + LANES]
    return total


def kernel(
    sizes,
    live_ref, blocks_ref, count_ref, owner_ref,
    section_ref, entering_ref, grad_ref, arriving_ref, stash_ref, gain_ref,
    up_hbm, down_hbm,
    outputs_ref, grads_ref, owned_ref, filled_ref,
    up_ref, down_ref,
    src_a, src_b, all_a, all_b, src_f, src_d, all_f, all_d,
    sent_p0, sent_a0, sent_f0, sent_p1, sent_a1, sent_f1,
    got_p0, got_a0, got_f0, got_p1, got_a1, got_f1,
    mix_s0, mix_h0, mix_f0, mix_h1, mix_s1, mix_f1,
    keep_b0, keep_f0, keep_b1, keep_f1,
    half_b0, half_f0, half_b1, half_f1,
    other_b0, other_f0, other_b1, other_f1,
    chip_b0, chip_f0, chip_b1, chip_f1,
    rows_b0, rows_f0, rows_b1, rows_f1,
    left_table, right_table, block_buf, send_buf, recv_buf,
    held_p1, held_scale1,
    weight_sem,
    gather_send, gather_recv,
    tensor_send, tensor_recv,
    reduce_send, reduce_recv,
    block_send, block_recv,
):
    ns, nz, nt = sizes
    nd = 2 * nz
    local, width = section_ref.shape
    hidden = up_ref.shape[1]
    rows = local * nd
    part = rows // nt
    dw = width * nt
    section = lax.axis_index("section")
    dp = lax.axis_index("dp")
    tensor = lax.axis_index("tensor")
    z = dp // 2
    core = dp % 2
    partner = (section, z * 2 + 1 - core, tensor)
    after = lax.rem(section + 1, ns)
    before = lax.rem(section + ns - 1, ns)

    def remote(src, dst, send_sem, recv_sem, device):
        return pltpu.make_async_remote_copy(
            src_ref=src, dst_ref=dst, send_sem=send_sem, recv_sem=recv_sem,
            device_id=device, device_id_type=MESH,
        )

    def far_first(k):
        return nz // 2 + (1 - 2 * (k % 2)) * ((k + 1) // 2)

    def zup(j):
        return lax.rem(z + j, nz)

    def zdown(j):
        return lax.rem(z + nz - j, nz)

    def tup(j):
        return lax.rem(tensor + j, nt)

    def loop(lo, hi, fn):
        def step(k, carry):
            fn(k)
            return carry
        lax.fori_loop(lo, hi, step, 0)

    weights_up = pltpu.make_async_copy(up_hbm, up_ref, weight_sem.at[0])
    weights_down = pltpu.make_async_copy(down_hbm, down_ref, weight_sem.at[1])
    weights_up.start()
    weights_down.start()

    barrier = pltpu.get_barrier_semaphore()

    def greet(device):
        pl.semaphore_signal(barrier, inc=1, device_id=device, device_id_type=MESH)

    def greet_dp(k):
        greet((section, lax.rem(dp + k, nd), tensor))

    def greet_sections(k):
        greet((after, k * 2 + core, tensor))
        greet((before, k * 2 + core, tensor))

    loop(1, nd, greet_dp)
    for j in range(1, nt):
        greet((section, dp, tup(j)))
    loop(0, nz, greet_sections)

    src_a[0] = stash_ref[0]
    src_a[1] = grad_ref[...]
    src_b[0] = section_ref[...]
    src_b[1] = stash_ref[1]
    all_a[core, z] = src_a[...]
    all_b[core, z] = src_b[...]
    recv_buf[dp] = jnp.zeros(recv_buf.shape[1:], BF16)

    pl.semaphore_wait(barrier, (nd - 1) + (nt - 1) + 2 * nz)

    def gather_copy(g, src, dst, j, target):
        return remote(src, dst.at[core, z], gather_send.at[g, j], gather_recv.at[g, j], target)

    def gather_start(g, src, dst):
        def send(k):
            j = far_first(k)
            gather_copy(g, src, dst, j, (section, zup(j) * 2 + core, tensor)).start()
        loop(0, nz - 1, send)
        gather_copy(g, src, dst, nz, partner).start()

    def gather_next_start(g, src, dst, target_section):
        def send(k):
            j = far_first(k)
            gather_copy(g, src, dst, j, (target_section, zup(j) * 2 + core, tensor)).start()
        loop(0, nz, send)

    def relay_copy(g, dst, j):
        slot = dst.at[core, zdown(j)]
        return remote(slot, slot, gather_send.at[g, nz + j], gather_recv.at[g, nz + j], partner)

    def relay(g, dst, count):
        def forward(k):
            j = far_first(k)
            slot = dst.at[core, zdown(j)]
            remote(slot, slot, gather_send.at[g, j], gather_recv.at[g, j], partner).wait_recv()
            relay_copy(g, dst, j).start()
        loop(0, count, forward)

    def gather_wait(g, dst):
        def arrive(j):
            slot = dst.at[1 - core, zdown(j)]
            remote(slot, slot, gather_send.at[g, nz + j], gather_recv.at[g, nz + j], partner).wait_recv()
        loop(0, nz, arrive)

    def sum_copy(g, sent, got, j):
        return remote(
            sent.at[pl.ds(pl.multiple_of(tup(j) * part, part), part)], got.at[j],
            tensor_send.at[g, j], tensor_recv.at[g, j], (section, dp, tup(j)),
        )

    def sum_start(g, sent, got):
        for j in range(1, nt):
            sum_copy(g, sent, got, j).start()

    mine = pl.ds(pl.multiple_of(tensor * part, part), part)

    def sum_end(g, sent, got):
        total = sent[mine].astype(F32)
        for j in range(1, nt):
            sum_copy(g, sent, got, j).wait_recv()
            total = total + got[j].astype(F32)
        return total

    def share_copy(g, mix, j):
        return remote(
            mix.at[mine], mix.at[mine], tensor_send.at[g, j], tensor_recv.at[g, j], (section, dp, tup(j))
        )

    def share_start(g, mix):
        for j in range(1, nt):
            share_copy(g, mix, j).start()

    def share_wait(g, mix):
        for j in range(1, nt):
            share_copy(g, mix, j).wait_recv()

    def reduce_start(g, value, keep, half, other):
        keep[...] = value.reshape(2, rows // 2, width)
        half[...] = keep[1 - core].astype(BF16)
        remote(half, other, reduce_send.at[g, 0], reduce_recv.at[g, 0], partner).start()

    def chip_copy(g, chip, got, j):
        return remote(
            chip.at[zup(j)], got.at[z], reduce_send.at[g, j], reduce_recv.at[g, j],
            (section, zup(j) * 2 + core, tensor),
        )

    def reduce_middle(g, keep, half, other, chip, got):
        remote(half, other, reduce_send.at[g, 0], reduce_recv.at[g, 0], partner).wait_recv()
        total = keep[core] + other[...].astype(F32)
        chip[...] = total.reshape(nz, local, width).astype(BF16)
        got[z] = chip[z]

        def send(k):
            chip_copy(g, chip, got, far_first(k)).start()
        loop(0, nz - 1, send)

    def reduce_end(g, chip, got):
        def arrive(j):
            chip_copy(g, chip, got, j).wait_recv()
        loop(1, nz, arrive)
        return jnp.sum(got[...].astype(F32), axis=0)

    def flat_rows(ref):
        return ref[...].astype(F32).reshape(rows, width)

    gain = gain_ref[...].astype(F32)

    def scales_of(lane_squares):
        return lax.rsqrt(jnp.sum(lane_squares, axis=1, keepdims=True) / dw + EPSILON)

    def up_product(widened):
        normed = (widened * gain).astype(BF16)
        product = jnp.dot(normed, up_ref[...], preferred_element_type=F32)
        return normed, product.astype(BF16), lane_blocks_sum(widened * widened).astype(BF16)

    def to_table(table, first, turn, value):
        for b in range(value.shape[1] // BLK):
            table[first + b, turn * rows : (turn + 1) * rows, :] = value[:, b * BLK : (b + 1) * BLK]

    hidden_blocks = hidden // BLK
    channel_blocks = width // BLK
    F0, A_, B_, D1 = 0, 0, 1, 2

    gather_start(0, src_a, all_a)
    gather_start(1, src_b, all_b)

    relay(0, all_a, nz - 1)
    weights_up.wait()
    gather_wait(0, all_a)
    x0 = all_a[:, :, 0].astype(F32).reshape(rows, width)
    normed0, product0, squares0 = up_product(x0)
    sent_p0[:, :hidden] = product0
    sent_p0[:, hidden:] = squares0
    sum_start(0, sent_p0, got_p0)
    weights_down.wait()
    dy0 = all_a[:, :, 1].astype(F32).reshape(rows, width).astype(BF16)
    sent_a0[...] = times_transposed(dy0, down_ref[...]).astype(BF16)
    sum_start(1, sent_a0, got_a0)
    to_table(left_table, 0, 0, normed0)
    to_table(right_table, hidden_blocks, 0, dy0)

    relay(1, all_b, nz - 1)
    gather_wait(1, all_b)
    f0 = all_b[:, :, 0].astype(F32).reshape(rows, width)
    _, product_f0, squares_f0 = up_product(f0)
    sent_f0[:, :hidden] = product_f0
    sent_f0[:, hidden:] = squares_f0
    sum_start(2, sent_f0, got_f0)
    x1 = all_b[:, :, 1].astype(F32).reshape(rows, width)
    normed1, product1, squares1 = up_product(x1)
    sent_p1[:, :hidden] = product1
    sent_p1[:, hidden:] = squares1
    to_table(left_table, 0, 1, normed1)

    def backward_middle(total_p, total_a, mix):
        product, scales = total_p
        inner = product * scales
        gate = jax.nn.sigmoid(inner)
        hidden_grad = total_a * gate * (1.0 + inner * (1.0 - gate))
        mix[mine, :hidden] = (hidden_grad * scales).astype(BF16)
        per_lane = lane_blocks_sum(hidden_grad * product)
        mix[mine, hidden:] = (per_lane * (scales * scales * scales / dw)).astype(BF16)

    def activated_of(product, scales):
        inner = product * scales
        return (inner * jax.nn.sigmoid(inner)).astype(BF16)

    def product_end(g, sent, got):
        total = sum_end(g, sent, got)
        return total[:, :hidden], scales_of(total[:, hidden:])

    total_p0 = product_end(0, sent_p0, got_p0)
    total_a0 = sum_end(1, sent_a0, got_a0)
    backward_middle(total_p0, total_a0, mix_s0)
    share_start(6, mix_s0)
    sum_start(3, sent_p1, got_p1)

    total_f0 = product_end(2, sent_f0, got_f0)
    mix_f0[mine] = activated_of(*total_f0)
    share_start(7, mix_f0)
    mix_h0[mine] = activated_of(*total_p0)
    share_start(8, mix_h0)

    def normed_grad(mix, widened):
        part_sum = times_transposed(mix[:, :hidden], up_ref[...])
        coefficient = jnp.sum(mix[:, hidden:].astype(F32), axis=1, keepdims=True)
        return part_sum * gain - coefficient * widened

    share_wait(6, mix_s0)
    reduce_start(0, normed_grad(mix_s0, all_a[:, :, 0].astype(F32).reshape(rows, width)), keep_b0, half_b0, other_b0)
    to_table(right_table, 0, 0, mix_s0[:, :hidden])

    share_wait(7, mix_f0)
    reduce_start(1, jnp.dot(mix_f0[...], down_ref[...], preferred_element_type=F32), keep_f0, half_f0, other_f0)
    reduce_middle(0, keep_b0, half_b0, other_b0, chip_b0, rows_b0)
    reduce_middle(1, keep_f0, half_f0, other_f0, chip_f0, rows_f0)

    total_p1, scales1 = product_end(3, sent_p1, got_p1)
    held_p1[...] = total_p1
    held_scale1[...] = jnp.broadcast_to(scales1, held_scale1.shape)
    mix_h1[mine] = activated_of(total_p1, scales1)
    share_start(9, mix_h1)

    row_ids = dp * local + lax.broadcasted_iota(jnp.int32, (local, width), 0)
    masked = jnp.where(row_ids < live_ref[0], arriving_ref[...].astype(F32), 0.0)
    input_grad0 = (src_a[1].astype(F32) + reduce_end(0, chip_b0, rows_b0))
    grads_ref[0] = input_grad0.astype(BF16)
    src_d[...] = jnp.where(section == 0, masked, input_grad0).astype(BF16)
    gather_next_start(2, src_d, all_d, before)

    output0 = src_b[0].astype(F32) + reduce_end(1, chip_f0, rows_f0)
    outputs_ref[0] = output0.astype(BF16)
    src_f[...] = jnp.where(section == ns - 1, entering_ref[...].astype(F32), output0).astype(BF16)
    gather_next_start(3, src_f, all_f, after)

    share_wait(8, mix_h0)
    to_table(left_table, channel_blocks, 0, mix_h0[...])
    share_wait(9, mix_h1)
    to_table(left_table, channel_blocks, 1, mix_h1[...])

    capacity = owner_ref.shape[1]
    up_count = hidden_blocks * channel_blocks
    left_index, right_index = [], []
    for k in range(capacity):
        number = blocks_ref[dp, k]
        down_number = jnp.maximum(number - up_count, 0)
        is_up = number < up_count
        left_index.append(
            jnp.where(is_up, number // hidden_blocks, channel_blocks + down_number // channel_blocks)
        )
        right_index.append(
            jnp.where(is_up, number % hidden_blocks, hidden_blocks + down_number % channel_blocks)
        )
    my_count = count_ref[dp]
    my_owners = [owner_ref[dp, k] for k in range(capacity)]
    picks = []
    for o in range(nd):
        pick = jnp.int32(0)
        for k in range(capacity):
            pick = jnp.where((my_owners[k] == o) & (k < my_count), k, pick)
        picks.append(pick)
    taken = jnp.int32(0)
    sources = [jnp.int32(0) for _ in range(capacity)]
    for h in range(nd):
        sends = jnp.int32(0)
        for k in range(capacity):
            sends = jnp.where((owner_ref[h, k] == dp) & (k < count_ref[h]), 1, sends)
        for i in range(capacity):
            sources[i] = jnp.where((sends == 1) & (taken == i), h, sources[i])
        taken = taken + sends

    relay(2, all_d, nz)
    gather_wait(2, all_d)
    dy1 = flat_rows(all_d).astype(BF16)
    sent_a1[...] = times_transposed(dy1, down_ref[...]).astype(BF16)
    sum_start(4, sent_a1, got_a1)
    to_table(right_table, hidden_blocks, 1, dy1)

    relay(3, all_f, nz)
    gather_wait(3, all_f)
    f1 = flat_rows(all_f)
    _, product_f1, squares_f1 = up_product(f1)
    sent_f1[:, :hidden] = product_f1
    sent_f1[:, hidden:] = squares_f1
    sum_start(5, sent_f1, got_f1)

    total_a1 = sum_end(4, sent_a1, got_a1)
    backward_middle((held_p1[...], held_scale1[:, :1]), total_a1, mix_s1)
    share_start(10, mix_s1)

    total_f1 = product_end(5, sent_f1, got_f1)
    mix_f1[mine] = activated_of(*total_f1)
    share_start(11, mix_f1)

    share_wait(10, mix_s1)
    to_table(right_table, 0, 1, mix_s1[:, :hidden])
    for k in range(capacity):
        block = lax.dot_general(
            left_table[left_index[k]], right_table[right_index[k]],
            (((0,), (0,)), ((), ())), preferred_element_type=F32,
        )
        block_buf[k] = block.astype(BF16)
    for o in range(nd):
        send_buf[o] = block_buf[picks[o]]

    def block_copy(j):
        owner = lax.rem(dp + j, nd)
        return remote(
            send_buf.at[owner], recv_buf.at[dp], block_send.at[j], block_recv.at[j],
            (section, owner, tensor),
        )

    def send_block(k):
        block_copy(nz + (1 - 2 * (k % 2)) * ((k + 1) // 2)).start()
    loop(0, nd - 1, send_block)

    reduce_start(2, normed_grad(mix_s1, all_b[:, :, 1].astype(F32).reshape(rows, width)), keep_b1, half_b1, other_b1)
    share_wait(11, mix_f1)
    reduce_start(3, jnp.dot(mix_f1[...], down_ref[...], preferred_element_type=F32), keep_f1, half_f1, other_f1)
    reduce_middle(2, keep_b1, half_b1, other_b1, chip_b1, rows_b1)
    reduce_middle(3, keep_f1, half_f1, other_f1, chip_f1, rows_f1)
    grads_ref[1] = (all_d[core, z].astype(F32) + reduce_end(2, chip_b1, rows_b1)).astype(BF16)
    outputs_ref[1] = (all_f[core, z].astype(F32) + reduce_end(3, chip_f1, rows_f1)).astype(BF16)

    def got_block(j):
        source = lax.rem(dp + nd - j, nd)
        remote(
            send_buf.at[source], recv_buf.at[source], block_send.at[j], block_recv.at[j],
            (section, source, tensor),
        ).wait_recv()
    loop(1, nd, got_block)
    for i in range(capacity):
        owned_ref[i] = jnp.where(i < taken, recv_buf[sources[i]].astype(F32), 0.0)
        filled_ref[i] = jnp.where(i < taken, jnp.ones((1, LANES), F32), 0.0)

    for g, src, dst in ((0, src_a, all_a), (1, src_b, all_b)):
        def left_gather(j, g=g, src=src, dst=dst):
            gather_copy(g, src, dst, j, partner).wait_send()
            relay_copy(g, dst, j).wait_send()
        loop(1, nz, left_gather)
        gather_copy(g, src, dst, nz, partner).wait_send()
    for g, src, dst in ((2, src_d, all_d), (3, src_f, all_f)):
        def left_next(j, g=g, src=src, dst=dst):
            gather_copy(g, src, dst, j, partner).wait_send()
            relay_copy(g, dst, j).wait_send()
        loop(0, nz, left_next)
    for g, sent, got in (
        (0, sent_p0, got_p0), (1, sent_a0, got_a0), (2, sent_f0, got_f0),
        (3, sent_p1, got_p1), (4, sent_a1, got_a1), (5, sent_f1, got_f1),
    ):
        for j in range(1, nt):
            sum_copy(g, sent, got, j).wait_send()
    for g, mix in ((6, mix_s0), (7, mix_f0), (8, mix_h0), (9, mix_h1), (10, mix_s1), (11, mix_f1)):
        for j in range(1, nt):
            share_copy(g, mix, j).wait_send()
    for g, half, other, chip, got in (
        (0, half_b0, other_b0, chip_b0, rows_b0), (1, half_f0, other_f0, chip_f0, rows_f0),
        (2, half_b1, other_b1, chip_b1, rows_b1), (3, half_f1, other_f1, chip_f1, rows_f1),
    ):
        remote(half, other, reduce_send.at[g, 0], reduce_recv.at[g, 0], partner).wait_send()
        def left_reduce(j, g=g, chip=chip, got=got):
            chip_copy(g, chip, got, j).wait_send()
        loop(1, nz, left_reduce)

    def left_block(j):
        block_copy(j).wait_send()
    loop(1, nd, left_block)


def body(
    sizes,
    section_inputs, entering, grad_outputs, arriving, live_rows, stashed_inputs, norm_gain,
    up_weight, down_weight, held_blocks, held_count, held_owner, first_moment, second_moment,
):
    ns, nz, nt = sizes
    nd = 2 * nz
    local, width = section_inputs.shape[1:]
    hidden = up_weight.shape[2]
    rows = local * nd
    part = rows // nt
    capacity = held_owner.shape[3]
    turns = stashed_inputs.shape[1]
    blocks = hidden // BLK + width // BLK
    smem = pl.BlockSpec(memory_space=pltpu.SMEM)
    vmem = pl.BlockSpec(memory_space=pltpu.VMEM)
    anywhere = pl.BlockSpec(memory_space=pl.ANY)
    wide = hidden + LANES

    def several(count, shape, dtype):
        return [pltpu.VMEM(shape, dtype) for _ in range(count)]

    scratch = [
        pltpu.VMEM((width, hidden), BF16), pltpu.VMEM((hidden, width), BF16),
        *several(2, (2, local, width), BF16),
        *several(2, (2, nz, 2, local, width), BF16),
        *several(2, (local, width), BF16),
        *several(2, (2, nz, local, width), BF16),
        *[pltpu.VMEM((rows, w), BF16) for w in (wide, hidden, wide, wide, hidden, wide)],
        *[pltpu.VMEM((nt, part, w), BF16) for w in (wide, hidden, wide, wide, hidden, wide)],
        *[pltpu.VMEM((rows, w), BF16) for w in (wide, hidden, hidden, hidden, wide, hidden)],
        *several(4, (2, rows // 2, width), F32),
        *several(4, (rows // 2, width), BF16),
        *several(4, (rows // 2, width), BF16),
        *several(4, (nz, local, width), BF16),
        *several(4, (nz, local, width), BF16),
        *several(2, (blocks, turns * rows, BLK), BF16),
        pltpu.VMEM((capacity, BLK, BLK), BF16),
        *several(2, (nd, BLK, BLK), BF16),
        pltpu.VMEM((part, hidden), F32), pltpu.VMEM((part, LANES), F32),
        pltpu.SemaphoreType.DMA((2,)),
        pltpu.SemaphoreType.DMA((4, 2 * nz)), pltpu.SemaphoreType.DMA((4, 2 * nz)),
        pltpu.SemaphoreType.DMA((12, nt)), pltpu.SemaphoreType.DMA((12, nt)),
        pltpu.SemaphoreType.DMA((4, nz)), pltpu.SemaphoreType.DMA((4, nz)),
        pltpu.SemaphoreType.DMA((nd,)), pltpu.SemaphoreType.DMA((nd,)),
    ]
    outputs, grads, owned, filled = pl.pallas_call(
        functools.partial(kernel, sizes),
        out_shape=(
            jax.ShapeDtypeStruct((turns, local, width), BF16),
            jax.ShapeDtypeStruct((turns, local, width), BF16),
            jax.ShapeDtypeStruct((capacity, BLK, BLK), F32),
            jax.ShapeDtypeStruct((capacity, 1, LANES), F32),
        ),
        in_specs=[smem] * 4 + [vmem] * 6 + [anywhere] * 2,
        out_specs=[vmem] * 4,
        scratch_shapes=scratch,
        compiler_params=pltpu.CompilerParams(
            collective_id=0, has_side_effects=True, vmem_limit_bytes=56 * 1024 * 1024
        ),
        name="relay",
    )(
        live_rows, held_blocks[0, 0], held_count[0, 0], held_owner[0, 0],
        section_inputs[0], entering[0], grad_outputs[0], arriving[0], stashed_inputs[0], norm_gain,
        up_weight[0], down_weight[0],
    )
    is_filled = filled[:, :, :1] > 0.5
    first_new = 0.9 * first_moment[0, 0, 0] + 0.1 * owned
    second_new = 0.999 * second_moment[0, 0, 0] + 0.001 * owned * owned
    direction = first_new / (jnp.sqrt(second_new) + 1e-08)
    first_out = jnp.where(is_filled, first_new, 0.0)
    second_out = jnp.where(is_filled, second_new, 0.0)
    direction_out = jnp.where(is_filled, direction, 0.0)
    return (
        outputs[None], grads[None],
        first_out[None, None, None], second_out[None, None, None], direction_out[None, None, None],
    )


def solution(mesh):
    sizes = (mesh.shape["section"], mesh.shape["dp"] // 2, mesh.shape["tensor"])
    return jax.shard_map(
        functools.partial(body, sizes),
        mesh=mesh,
        in_specs=(
            P("section", "dp", "tensor"),
            P(None, "dp", "tensor"),
            P("section", "dp", "tensor"),
            P(None, "dp", "tensor"),
            P(),
            P("section", None, "dp", "tensor"),
            P("section", "tensor"),
            P("section", "tensor", "dp"),
            P("section", "dp", "tensor"),
            P("section", "tensor", None, None),
            P("section", "tensor", None),
            P("section", "tensor", None, None),
            P("section", "tensor", "dp", None, None, None),
            P("section", "tensor", "dp", None, None, None),
        ),
        out_specs=(
            P("section", None, "dp", "tensor"),
            P("section", None, "dp", "tensor"),
            P("section", "tensor", "dp", None, None, None),
            P("section", "tensor", "dp", None, None, None),
            P("section", "tensor", "dp", None, None, None),
        ),
        check_vma=False,
    )
```

```python
import functools

import jax
import jax.numpy as jnp
from jax import lax
from jax.experimental import pallas as pl
from jax.experimental.pallas import tpu as pltpu
from jax.sharding import PartitionSpec as P

MESH = pl.DeviceIdType.MESH
BLK = 128
LANES = 128
EPSILON = 1e-06
F32 = jnp.float32
BF16 = jnp.bfloat16


def times_transposed(left, right):
    return lax.dot_general(left, right, (((1,), (1,)), ((), ())), preferred_element_type=F32)


def lane_blocks_sum(value):
    total = value[:, :LANES]
    for start in range(LANES, value.shape[1], LANES):
        total = total + value[:, start : start + LANES]
    return total


def kernel(
    sizes,
    live_ref, blocks_ref, count_ref, owner_ref,
    section_hbm, entering_hbm, grad_hbm, arriving_hbm, stash_hbm, gain_hbm,
    up_hbm, down_hbm,
    outputs_ref, grads_ref, owned_ref, filled_ref,
    up_ref, down_ref,
    entering_ref, arriving_ref, gain_ref,
    src_a, src_b, all_a, all_b, src_f, src_d, all_f, all_d,
    sent_p0, sent_a0, sent_f0, sent_p1, sent_a1, sent_f1,
    got_p0, got_a0, got_f0, got_p1, got_a1, got_f1,
    mix_s0, mix_h0, mix_f0, mix_h1, mix_s1, mix_f1,
    keep_f0, keep_b1, keep_f1,
    half_f0, half_b1, half_f1,
    other_f0, other_b1, other_f1,
    chip_f0, chip_b1, chip_f1,
    rows_f0, rows_b1, rows_f1,
    parts_b0, rows_b0,
    left_table, right_table, block_buf, send_buf, recv_buf,
    held_p1, held_scale1,
    weight_sem, input_sem,
    gather_send, gather_recv,
    tensor_send, tensor_recv,
    reduce_send, reduce_recv,
    block_send, block_recv,
):
    ns, nz, nt = sizes
    nd = 2 * nz
    local, width = entering_ref.shape
    hidden = up_ref.shape[1]
    rows = local * nd
    part = rows // nt
    dw = width * nt
    section = lax.axis_index("section")
    dp = lax.axis_index("dp")
    tensor = lax.axis_index("tensor")
    z = dp // 2
    core = dp % 2
    partner = (section, z * 2 + 1 - core, tensor)
    after = lax.rem(section + 1, ns)
    before = lax.rem(section + ns - 1, ns)

    leaving = []
    coming = {}

    def remote(src, dst, send_sem, recv_sem, device):
        return pltpu.make_async_remote_copy(
            src_ref=src, dst_ref=dst, send_sem=send_sem, recv_sem=recv_sem,
            device_id=device, device_id_type=MESH,
        )

    def far_first(k):
        return nz // 2 + (1 - 2 * (k % 2)) * ((k + 1) // 2)

    def zup(j):
        return lax.rem(z + j, nz)

    def zdown(j):
        return lax.rem(z + nz - j, nz)

    def tup(j):
        return lax.rem(tensor + j, nt)

    def loop(lo, hi, fn):
        def step(k, carry):
            fn(k)
            return carry
        lax.fori_loop(lo, hi, step, 0)

    weights_up = pltpu.make_async_copy(up_hbm, up_ref, weight_sem.at[0])
    weights_down = pltpu.make_async_copy(down_hbm, down_ref, weight_sem.at[1])

    barrier = pltpu.get_barrier_semaphore()

    def greet(device):
        pl.semaphore_signal(barrier, inc=1, device_id=device, device_id_type=MESH)

    def greet_dp(k):
        greet((section, lax.rem(dp + k, nd), tensor))

    def greet_sections(k):
        greet((after, k * 2 + core, tensor))
        greet((before, k * 2 + core, tensor))

    loop(1, nd, greet_dp)
    for j in range(1, nt):
        greet((section, dp, tup(j)))
    loop(0, nz, greet_sections)

    inputs = [
        pltpu.make_async_copy(src, dst, input_sem.at[i])
        for i, (src, dst) in enumerate((
            (stash_hbm.at[0], src_a.at[0]), (grad_hbm, src_a.at[1]),
            (section_hbm, src_b.at[0]), (stash_hbm.at[1], src_b.at[1]),
            (stash_hbm.at[0], all_a.at[core, z, 0]), (grad_hbm, all_a.at[core, z, 1]),
            (section_hbm, all_b.at[core, z, 0]), (stash_hbm.at[1], all_b.at[core, z, 1]),
            (entering_hbm, entering_ref), (arriving_hbm, arriving_ref), (gain_hbm, gain_ref),
        ))
    ]
    for copy in inputs:
        copy.start()
    weights_up.start()
    weights_down.start()
    for copy in inputs:
        copy.wait()
    recv_buf[dp] = jnp.zeros(recv_buf.shape[1:], BF16)

    pl.semaphore_wait(barrier, (nd - 1) + (nt - 1) + 2 * nz)

    def gather_copy(g, src, dst, j, target):
        return remote(src, dst.at[core, z], gather_send.at[g, j], gather_recv.at[g, j], target)

    def gather_start(g, src, dst):
        def send(k):
            j = far_first(k)
            gather_copy(g, src, dst, j, (section, zup(j) * 2 + core, tensor)).start()
        loop(0, nz - 1, send)
        gather_copy(g, src, dst, nz, partner).start()

        def left(j):
            gather_copy(g, src, dst, j, partner).wait_send()
        leaving.append(lambda: loop(1, nz + 1, left))
        coming["gather", g] = lambda: (relay(g, dst, nz - 1), gather_wait(g, dst))

    def gather_next_start(g, src, dst, target_section):
        def send(k):
            j = far_first(k)
            gather_copy(g, src, dst, j, (target_section, zup(j) * 2 + core, tensor)).start()
        loop(0, nz, send)

        def left(j):
            gather_copy(g, src, dst, j, partner).wait_send()
        leaving.append(lambda: loop(0, nz, left))
        coming["gather", g] = lambda: (relay(g, dst, nz), gather_wait(g, dst))

    def relay_copy(g, dst, j):
        slot = dst.at[core, zdown(j)]
        return remote(slot, slot, gather_send.at[g, nz + j], gather_recv.at[g, nz + j], partner)

    def relay(g, dst, count):
        def forward(k):
            j = far_first(k)
            slot = dst.at[core, zdown(j)]
            remote(slot, slot, gather_send.at[g, j], gather_recv.at[g, j], partner).wait_recv()
            relay_copy(g, dst, j).start()
        loop(0, count, forward)

        def left(j):
            relay_copy(g, dst, j).wait_send()
        leaving.append(lambda: loop(nz - count, nz, left))

    def gather_wait(g, dst):
        coming.pop(("gather", g))

        def arrive(j):
            slot = dst.at[1 - core, zdown(j)]
            remote(slot, slot, gather_send.at[g, nz + j], gather_recv.at[g, nz + j], partner).wait_recv()
        loop(0, nz, arrive)

    def both_copy(g, src, dst, j, other_core, target_section):
        return remote(
            src, dst.at[core, z],
            gather_send.at[g, 2 * j + other_core], gather_recv.at[g, 2 * j + other_core],
            (target_section, zup(j) * 2 + lax.rem(core + other_core, 2), tensor),
        )

    def both_start(g, src, dst, target_section):
        def send(k):
            j = far_first(k)
            both_copy(g, src, dst, j, 0, target_section).start()
            both_copy(g, src, dst, j, 1, target_section).start()
        loop(0, nz, send)

        def left(j):
            both_copy(g, src, dst, j, 0, target_section).wait_send()
            both_copy(g, src, dst, j, 1, target_section).wait_send()
        leaving.append(lambda: loop(0, nz, left))
        coming["both", g] = lambda: both_wait(g, dst)

    def both_wait(g, dst):
        coming.pop(("both", g))

        def arrive(j):
            for other_core in range(2):
                slot = dst.at[lax.rem(core + other_core, 2), zdown(j)]
                sem = 2 * j + other_core
                remote(slot, slot, gather_send.at[g, sem], gather_recv.at[g, sem], partner).wait_recv()
        loop(0, nz, arrive)

    def sum_copy(g, sent, got, j):
        return remote(
            sent.at[pl.ds(pl.multiple_of(tup(j) * part, part), part)], got.at[j],
            tensor_send.at[g, j], tensor_recv.at[g, j], (section, dp, tup(j)),
        )

    def sum_start(g, sent, got):
        for j in range(1, nt):
            sum_copy(g, sent, got, j).start()
            leaving.append(lambda j=j: sum_copy(g, sent, got, j).wait_send())
        coming["sum", g] = lambda: sum_end(g, sent, got)

    mine = pl.ds(pl.multiple_of(tensor * part, part), part)

    def sum_end(g, sent, got):
        coming.pop(("sum", g))
        total = sent[mine].astype(F32)
        for j in range(1, nt):
            sum_copy(g, sent, got, j).wait_recv()
            total = total + got[j].astype(F32)
        return total

    def share_copy(g, mix, j):
        return remote(
            mix.at[mine], mix.at[mine], tensor_send.at[g, j], tensor_recv.at[g, j], (section, dp, tup(j))
        )

    def share_start(g, mix):
        for j in range(1, nt):
            share_copy(g, mix, j).start()
            leaving.append(lambda j=j: share_copy(g, mix, j).wait_send())
        coming["share", g] = lambda: share_wait(g, mix)

    def share_wait(g, mix):
        coming.pop(("share", g))
        for j in range(1, nt):
            share_copy(g, mix, j).wait_recv()

    def reduce_start(g, value, keep, half, other):
        keep[...] = value.reshape(2, rows // 2, width)
        half[...] = keep[1 - core].astype(BF16)
        swap = remote(half, other, reduce_send.at[g, 0], reduce_recv.at[g, 0], partner)
        swap.start()
        leaving.append(swap.wait_send)
        coming["swap", g] = swap.wait_recv

    def chip_copy(g, chip, got, j):
        return remote(
            chip.at[zup(j)], got.at[z], reduce_send.at[g, j], reduce_recv.at[g, j],
            (section, zup(j) * 2 + core, tensor),
        )

    def reduce_middle(g, keep, half, other, chip, got):
        coming.pop(("swap", g))()
        total = keep[core] + other[...].astype(F32)
        chip[...] = total.reshape(nz, local, width).astype(BF16)
        got[z] = chip[z]

        def send(k):
            chip_copy(g, chip, got, far_first(k)).start()
        loop(0, nz - 1, send)

        def left(j):
            chip_copy(g, chip, got, j).wait_send()
        leaving.append(lambda: loop(1, nz, left))
        coming["reduce", g] = lambda: reduce_end(g, chip, got)

    def reduce_end(g, chip, got):
        coming.pop(("reduce", g))

        def arrive(j):
            chip_copy(g, chip, got, j).wait_recv()
        loop(1, nz, arrive)
        return jnp.sum(got[...].astype(F32), axis=0)

    def scatter_copy(g, parts, got, j, other_core):
        target = lax.rem(core + other_core, 2)
        return remote(
            parts.at[target, zup(j)], got.at[dp],
            reduce_send.at[g, 2 * j + other_core], reduce_recv.at[g, 2 * j + other_core],
            (section, zup(j) * 2 + target, tensor),
        )

    def scatter_start(g, value, parts, got):
        parts[...] = value.reshape(parts.shape).astype(BF16)
        got[dp] = parts[core, z]

        def send(k):
            j = far_first(k)
            scatter_copy(g, parts, got, j, 0).start()
            scatter_copy(g, parts, got, j, 1).start()
        loop(0, nz - 1, send)
        scatter_copy(g, parts, got, 0, 1).start()

        def left(j):
            scatter_copy(g, parts, got, j, 0).wait_send()
            scatter_copy(g, parts, got, j, 1).wait_send()
        leaving.append(lambda: loop(1, nz, left))
        leaving.append(lambda: scatter_copy(g, parts, got, 0, 1).wait_send())
        coming["scatter", g] = lambda: scatter_end(g, parts, got)

    def scatter_end(g, parts, got):
        coming.pop(("scatter", g))

        def arrive(j, other_core):
            slot = got.at[zdown(j) * 2 + lax.rem(core + other_core, 2)]
            sem = 2 * j + other_core
            remote(slot, slot, reduce_send.at[g, sem], reduce_recv.at[g, sem], partner).wait_recv()

        def arrive_both(j):
            arrive(j, 0)
            arrive(j, 1)
        loop(1, nz, arrive_both)
        arrive(0, 1)
        return jnp.sum(got[...].astype(F32), axis=0)

    def flat_rows(ref):
        return ref[...].astype(F32).reshape(rows, width)

    gain = gain_ref[...].astype(F32)

    def scales_of(lane_squares):
        return lax.rsqrt(jnp.sum(lane_squares, axis=1, keepdims=True) / dw + EPSILON)

    def up_product(widened):
        normed = (widened * gain).astype(BF16)
        product = jnp.dot(normed, up_ref[...], preferred_element_type=F32)
        return normed, product.astype(BF16), lane_blocks_sum(widened * widened).astype(BF16)

    def to_table(table, first, turn, value):
        for b in range(value.shape[1] // BLK):
            table[first + b, turn * rows : (turn + 1) * rows, :] = value[:, b * BLK : (b + 1) * BLK]

    hidden_blocks = hidden // BLK
    channel_blocks = width // BLK

    def backward_middle(total_p, total_a, mix):
        product, scales = total_p
        inner = product * scales
        gate = jax.nn.sigmoid(inner)
        hidden_grad = total_a * gate * (1.0 + inner * (1.0 - gate))
        mix[mine, :hidden] = (hidden_grad * scales).astype(BF16)
        per_lane = lane_blocks_sum(hidden_grad * product)
        mix[mine, hidden:] = (per_lane * (scales * scales * scales / dw)).astype(BF16)

    def activated_of(product, scales):
        inner = product * scales
        return (inner * jax.nn.sigmoid(inner)).astype(BF16)

    def product_end(g, sent, got):
        total = sum_end(g, sent, got)
        return total[:, :hidden], scales_of(total[:, hidden:])

    def normed_grad(mix, widened):
        part_sum = times_transposed(mix[:, :hidden], up_ref[...])
        coefficient = jnp.sum(mix[:, hidden:].astype(F32), axis=1, keepdims=True)
        return part_sum * gain - coefficient * widened

    def stored_product(ref, product, lane_squares):
        ref[:, :hidden] = product
        ref[:, hidden:] = lane_squares

    def rows_of(ref, which):
        return ref[:, :, which].astype(F32).reshape(rows, width)

    gather_start(0, src_a, all_a)
    gather_start(1, src_b, all_b)

    relay(0, all_a, nz - 1)
    weights_up.wait()
    gather_wait(0, all_a)
    normed0, *made = up_product(rows_of(all_a, 0))
    stored_product(sent_p0, *made)
    sum_start(0, sent_p0, got_p0)
    weights_down.wait()
    dy0 = rows_of(all_a, 1).astype(BF16)
    sent_a0[...] = times_transposed(dy0, down_ref[...]).astype(BF16)
    sum_start(1, sent_a0, got_a0)
    to_table(left_table, 0, 0, normed0)
    to_table(right_table, hidden_blocks, 0, dy0)

    relay(1, all_b, nz - 1)
    gather_wait(1, all_b)
    normed, product, lane_squares = up_product(jnp.concatenate([rows_of(all_b, 0), rows_of(all_b, 1)]))
    stored_product(sent_f0, product[:rows], lane_squares[:rows])
    sum_start(2, sent_f0, got_f0)
    stored_product(sent_p1, product[rows:], lane_squares[rows:])
    to_table(left_table, 0, 1, normed[rows:])

    total_p0 = product_end(0, sent_p0, got_p0)
    total_a0 = sum_end(1, sent_a0, got_a0)
    backward_middle(total_p0, total_a0, mix_s0)
    share_start(6, mix_s0)

    total_f0 = product_end(2, sent_f0, got_f0)
    mix_f0[mine] = activated_of(*total_f0)
    share_start(7, mix_f0)
    mix_h0[mine] = activated_of(*total_p0)

    share_wait(6, mix_s0)
    scatter_start(0, normed_grad(mix_s0, rows_of(all_a, 0)), parts_b0, rows_b0)
    sum_start(3, sent_p1, got_p1)
    share_start(8, mix_h0)
    to_table(right_table, 0, 0, mix_s0[:, :hidden])

    share_wait(7, mix_f0)
    reduce_start(1, jnp.dot(mix_f0[...], down_ref[...], preferred_element_type=F32), keep_f0, half_f0, other_f0)
    reduce_middle(1, keep_f0, half_f0, other_f0, chip_f0, rows_f0)

    row_ids = dp * local + lax.broadcasted_iota(jnp.int32, (local, width), 0)
    masked = jnp.where(row_ids < live_ref[0], arriving_ref[...].astype(F32), 0.0)
    input_grad0 = src_a[1].astype(F32) + scatter_end(0, parts_b0, rows_b0)
    src_d[...] = jnp.where(section == 0, masked, input_grad0).astype(BF16)
    both_start(2, src_d, all_d, before)
    grads_ref[0] = input_grad0.astype(BF16)

    total_p1, scales1 = product_end(3, sent_p1, got_p1)
    held_p1[...] = total_p1
    held_scale1[...] = jnp.broadcast_to(scales1, held_scale1.shape)
    mix_h1[mine] = activated_of(total_p1, scales1)
    share_start(9, mix_h1)

    output0 = src_b[0].astype(F32) + reduce_end(1, chip_f0, rows_f0)
    src_f[...] = jnp.where(section == ns - 1, entering_ref[...].astype(F32), output0).astype(BF16)
    gather_next_start(3, src_f, all_f, after)
    outputs_ref[0] = output0.astype(BF16)

    share_wait(8, mix_h0)
    to_table(left_table, channel_blocks, 0, mix_h0[...])

    capacity = owner_ref.shape[0]
    up_count = hidden_blocks * channel_blocks
    left_index, right_index = [], []
    for k in range(capacity):
        number = blocks_ref[k, 0, dp]
        down_number = jnp.maximum(number - up_count, 0)
        is_up = number < up_count
        left_index.append(
            jnp.where(is_up, number // hidden_blocks, channel_blocks + down_number // channel_blocks)
        )
        right_index.append(
            jnp.where(is_up, number % hidden_blocks, hidden_blocks + down_number % channel_blocks)
        )
    my_count = count_ref[dp]
    my_owners = [owner_ref[k, 0, dp] for k in range(capacity)]
    picks = []
    for o in range(nd):
        pick = jnp.int32(0)
        for k in range(capacity):
            pick = jnp.where((my_owners[k] == o) & (k < my_count), k, pick)
        picks.append(pick)
    taken = jnp.int32(0)
    sources = [jnp.int32(0) for _ in range(capacity)]
    for h in range(nd):
        sends = jnp.int32(0)
        for k in range(capacity):
            sends = jnp.where((owner_ref[k, 0, h] == dp) & (k < count_ref[h]), 1, sends)
        for i in range(capacity):
            sources[i] = jnp.where((sends == 1) & (taken == i), h, sources[i])
        taken = taken + sends

    both_wait(2, all_d)
    dy1 = flat_rows(all_d).astype(BF16)
    sent_a1[...] = times_transposed(dy1, down_ref[...]).astype(BF16)
    sum_start(4, sent_a1, got_a1)
    to_table(right_table, hidden_blocks, 1, dy1)
    share_wait(9, mix_h1)
    to_table(left_table, channel_blocks, 1, mix_h1[...])

    relay(3, all_f, nz)
    gather_wait(3, all_f)
    _, *made = up_product(flat_rows(all_f))
    stored_product(sent_f1, *made)
    sum_start(5, sent_f1, got_f1)

    total_a1 = sum_end(4, sent_a1, got_a1)
    backward_middle((held_p1[...], held_scale1[:, :1]), total_a1, mix_s1)
    share_start(10, mix_s1)

    total_f1 = product_end(5, sent_f1, got_f1)
    mix_f1[mine] = activated_of(*total_f1)
    share_start(11, mix_f1)

    share_wait(10, mix_s1)
    to_table(right_table, 0, 1, mix_s1[:, :hidden])
    for k in range(capacity):
        block = lax.dot_general(
            left_table[left_index[k]], right_table[right_index[k]],
            (((0,), (0,)), ((), ())), preferred_element_type=F32,
        )
        block_buf[k] = block.astype(BF16)
    for o in range(nd):
        send_buf[o] = block_buf[picks[o]]

    def block_copy(j):
        owner = lax.rem(dp + j, nd)
        return remote(
            send_buf.at[owner], recv_buf.at[dp], block_send.at[j], block_recv.at[j],
            (section, owner, tensor),
        )

    def send_block(k):
        block_copy(nz + (1 - 2 * (k % 2)) * ((k + 1) // 2)).start()
    loop(0, nd - 1, send_block)

    def left_block(j):
        block_copy(j).wait_send()
    leaving.append(lambda: loop(1, nd, left_block))

    reduce_start(2, normed_grad(mix_s1, rows_of(all_b, 1)), keep_b1, half_b1, other_b1)
    share_wait(11, mix_f1)
    new_rows = jnp.dot(mix_f1[...], down_ref[...], preferred_element_type=F32)
    reduce_middle(2, keep_b1, half_b1, other_b1, chip_b1, rows_b1)
    reduce_start(3, new_rows, keep_f1, half_f1, other_f1)
    reduce_middle(3, keep_f1, half_f1, other_f1, chip_f1, rows_f1)
    grads_ref[1] = (all_d[core, z].astype(F32) + reduce_end(2, chip_b1, rows_b1)).astype(BF16)
    outputs_ref[1] = (all_f[core, z].astype(F32) + reduce_end(3, chip_f1, rows_f1)).astype(BF16)

    def got_block(j):
        source = lax.rem(dp + nd - j, nd)
        remote(
            send_buf.at[source], recv_buf.at[source], block_send.at[j], block_recv.at[j],
            (section, source, tensor),
        ).wait_recv()
    loop(1, nd, got_block)
    for i in range(capacity):
        owned_ref[i] = jnp.where(i < taken, recv_buf[sources[i]].astype(F32), 0.0).astype(BF16)
        filled_ref[i] = jnp.where(i < taken, jnp.ones((1, LANES), F32), 0.0)

    for wait in leaving:
        wait()


def adam(
    outputs_in, grads_in, owned_ref, filled_ref, first_ref, second_ref,
    outputs_ref, grads_ref, first_out, second_out, direction_out,
):
    outputs_ref[...] = outputs_in[...]
    grads_ref[...] = grads_in[...]
    for i in range(owned_ref.shape[0]):
        grad = owned_ref[i].astype(F32)
        filled = filled_ref[i] > 0.5
        first = 0.9 * first_ref[i] + 0.1 * grad
        second = 0.999 * second_ref[i] + 0.001 * grad * grad
        first_out[i] = jnp.where(filled, first, 0.0)
        second_out[i] = jnp.where(filled, second, 0.0)
        direction_out[i] = jnp.where(filled, first / (jnp.sqrt(second) + 1e-08), 0.0)


def by_slot(lists):
    return jnp.transpose(lists, (0, 3, 1, 2))[0]


def body(
    sizes,
    section_inputs, entering, grad_outputs, arriving, live_rows, stashed_inputs, norm_gain,
    up_weight, down_weight, held_blocks, held_count, held_owner, first_moment, second_moment,
):
    ns, nz, nt = sizes
    nd = 2 * nz
    local, width = section_inputs.shape[1:]
    hidden = up_weight.shape[2]
    rows = local * nd
    part = rows // nt
    capacity = held_owner.shape[3]
    turns = stashed_inputs.shape[1]
    blocks = hidden // BLK + width // BLK
    smem = pl.BlockSpec(memory_space=pltpu.SMEM)
    vmem = pl.BlockSpec(memory_space=pltpu.VMEM)
    anywhere = pl.BlockSpec(memory_space=pl.ANY)
    wide = hidden + LANES

    def several(count, shape, dtype):
        return [pltpu.VMEM(shape, dtype) for _ in range(count)]

    scratch = [
        pltpu.VMEM((width, hidden), BF16), pltpu.VMEM((hidden, width), BF16),
        *several(2, (local, width), BF16), pltpu.VMEM((1, width), BF16),
        *several(2, (2, local, width), BF16),
        *several(2, (2, nz, 2, local, width), BF16),
        *several(2, (local, width), BF16),
        *several(2, (2, nz, local, width), BF16),
        *[pltpu.VMEM((rows, w), BF16) for w in (wide, hidden, wide, wide, hidden, wide)],
        *[pltpu.VMEM((nt, part, w), BF16) for w in (wide, hidden, wide, wide, hidden, wide)],
        *[pltpu.VMEM((rows, w), BF16) for w in (wide, hidden, hidden, hidden, wide, hidden)],
        *several(3, (2, rows // 2, width), F32),
        *several(3, (rows // 2, width), BF16),
        *several(3, (rows // 2, width), BF16),
        *several(3, (nz, local, width), BF16),
        *several(3, (nz, local, width), BF16),
        pltpu.VMEM((2, nz, local, width), BF16), pltpu.VMEM((nd, local, width), BF16),
        *several(2, (blocks, turns * rows, BLK), BF16),
        pltpu.VMEM((capacity, BLK, BLK), BF16),
        *several(2, (nd, BLK, BLK), BF16),
        pltpu.VMEM((part, hidden), F32), pltpu.VMEM((part, LANES), F32),
        pltpu.SemaphoreType.DMA((2,)), pltpu.SemaphoreType.DMA((11,)),
        pltpu.SemaphoreType.DMA((4, 2 * nz)), pltpu.SemaphoreType.DMA((4, 2 * nz)),
        pltpu.SemaphoreType.DMA((12, nt)), pltpu.SemaphoreType.DMA((12, nt)),
        pltpu.SemaphoreType.DMA((4, 2 * nz)), pltpu.SemaphoreType.DMA((4, 2 * nz)),
        pltpu.SemaphoreType.DMA((nd,)), pltpu.SemaphoreType.DMA((nd,)),
    ]
    outputs, grads, owned, filled = pl.pallas_call(
        functools.partial(kernel, sizes),
        out_shape=(
            jax.ShapeDtypeStruct((turns, local, width), BF16),
            jax.ShapeDtypeStruct((turns, local, width), BF16),
            jax.ShapeDtypeStruct((capacity, BLK, BLK), BF16),
            jax.ShapeDtypeStruct((capacity, 1, LANES), F32),
        ),
        in_specs=[smem] * 4 + [anywhere] * 8,
        out_specs=[vmem] * 4,
        scratch_shapes=scratch,
        compiler_params=pltpu.CompilerParams(
            collective_id=0, has_side_effects=True, vmem_limit_bytes=56 * 1024 * 1024
        ),
        name="relay",
    )(
        live_rows, by_slot(held_blocks), held_count[0, 0], by_slot(held_owner),
        section_inputs[0], entering[0], grad_outputs[0], arriving[0], stashed_inputs[0], norm_gain,
        up_weight[0], down_weight[0],
    )
    block_shape = jax.ShapeDtypeStruct((capacity, BLK, BLK), F32)
    outputs, grads, first_out, second_out, direction_out = pl.pallas_call(
        adam,
        out_shape=(
            jax.ShapeDtypeStruct(outputs.shape, BF16), jax.ShapeDtypeStruct(grads.shape, BF16),
            block_shape, block_shape, block_shape,
        ),
        in_specs=[vmem] * 6,
        out_specs=[vmem] * 5,
        name="adam",
    )(outputs, grads, owned, filled, first_moment[0, 0, 0], second_moment[0, 0, 0])
    return (
        outputs[None], grads[None],
        first_out[None, None, None], second_out[None, None, None], direction_out[None, None, None],
    )


def solution(mesh):
    sizes = (mesh.shape["section"], mesh.shape["dp"] // 2, mesh.shape["tensor"])
    return jax.shard_map(
        functools.partial(body, sizes),
        mesh=mesh,
        in_specs=(
            P("section", "dp", "tensor"),
            P(None, "dp", "tensor"),
            P("section", "dp", "tensor"),
            P(None, "dp", "tensor"),
            P(),
            P("section", None, "dp", "tensor"),
            P("section", "tensor"),
            P("section", "tensor", "dp"),
            P("section", "dp", "tensor"),
            P("section", "tensor", None, None),
            P("section", "tensor", None),
            P("section", "tensor", None, None),
            P("section", "tensor", "dp", None, None, None),
            P("section", "tensor", "dp", None, None, None),
        ),
        out_specs=(
            P("section", None, "dp", "tensor"),
            P("section", None, "dp", "tensor"),
            P("section", "tensor", "dp", None, None, None),
            P("section", "tensor", "dp", None, None, None),
            P("section", "tensor", "dp", None, None, None),
        ),
        check_vma=False,
    )
```

```python
import functools

import jax
import jax.numpy as jnp
from jax import lax
from jax.experimental import pallas as pl
from jax.experimental.pallas import tpu as pltpu
from jax.sharding import PartitionSpec as P

MESH = pl.DeviceIdType.MESH
BLK = 128
LANES = 128
EPSILON = 1e-06
F32 = jnp.float32
BF16 = jnp.bfloat16


def times_transposed(left, right):
    return lax.dot_general(left, right, (((1,), (1,)), ((), ())), preferred_element_type=F32)


def lane_blocks_sum(value):
    total = value[:, :LANES]
    for start in range(LANES, value.shape[1], LANES):
        total = total + value[:, start : start + LANES]
    return total


def kernel(
    sizes,
    live_hbm, blocks_hbm, count_hbm, owner_hbm,
    section_hbm, entering_hbm, grad_hbm, arriving_hbm, stash_hbm, gain_hbm,
    up_hbm, down_hbm,
    outputs_ref, grads_ref, owned_ref, filled_ref,
    up_ref, down_ref,
    live_ref, blocks_ref, count_ref, owner_ref,
    entering_ref, arriving_ref, gain_ref,
    src_f, src_d,
    all_a, all_s, all_x, all_f, all_d,
    sent_p0, sent_a0, sent_f0, sent_p1, sent_a1, sent_f1,
    got_p0, got_a0, got_f0, got_p1, got_a1, got_f1,
    mix_s0, mix_h0, mix_f0, mix_h1, mix_s1, mix_f1,
    keep_f0, keep_b1, keep_f1,
    half_f0, half_b1, half_f1,
    other_f0, other_b1, other_f1,
    chip_f0, chip_b1, chip_f1,
    rows_f0, rows_b1, rows_f1,
    parts_b0, rows_b0,
    left_table, right_table, block_buf, send_buf, recv_buf,
    held_p1, held_scale1,
    weight_sem, input_sem,
    gather_send, gather_recv,
    tensor_send, tensor_recv,
    reduce_send, reduce_recv,
    block_send, block_recv,
):
    ns, nz, nt = sizes
    nd = 2 * nz
    local, width = entering_ref.shape
    hidden = up_ref.shape[1]
    rows = local * nd
    part = rows // nt
    dw = width * nt
    section = lax.axis_index("section")
    dp = lax.axis_index("dp")
    tensor = lax.axis_index("tensor")
    z = dp // 2
    core = dp % 2
    partner = (section, z * 2 + 1 - core, tensor)
    after = lax.rem(section + 1, ns)
    before = lax.rem(section + ns - 1, ns)

    leaving = []
    coming = {}

    def remote(src, dst, send_sem, recv_sem, device):
        return pltpu.make_async_remote_copy(
            src_ref=src, dst_ref=dst, send_sem=send_sem, recv_sem=recv_sem,
            device_id=device, device_id_type=MESH,
        )

    def far_first(k):
        return nz // 2 + (1 - 2 * (k % 2)) * ((k + 1) // 2)

    def zup(j):
        return lax.rem(z + j, nz)

    def zdown(j):
        return lax.rem(z + nz - j, nz)

    def tup(j):
        return lax.rem(tensor + j, nt)

    def loop(lo, hi, fn):
        def step(k, carry):
            fn(k)
            return carry
        lax.fori_loop(lo, hi, step, 0)

    weights_up = pltpu.make_async_copy(up_hbm, up_ref, weight_sem.at[0])
    weights_down = pltpu.make_async_copy(down_hbm, down_ref, weight_sem.at[1])

    barrier = pltpu.get_barrier_semaphore()

    def greet(device):
        pl.semaphore_signal(barrier, inc=1, device_id=device, device_id_type=MESH)

    def greet_dp(k):
        greet((section, lax.rem(dp + k, nd), tensor))

    def greet_sections(k):
        greet((after, k * 2 + core, tensor))
        greet((before, k * 2 + core, tensor))

    loop(1, nd, greet_dp)
    for j in range(1, nt):
        greet((section, dp, tup(j)))
    loop(0, nz, greet_sections)

    inputs = [
        pltpu.make_async_copy(src, dst, input_sem.at[i])
        for i, (src, dst) in enumerate((
            (stash_hbm.at[0], all_a.at[core, z, 0]), (grad_hbm, all_a.at[core, z, 1]),
            (section_hbm, all_s.at[core, z]), (stash_hbm.at[1], all_x.at[core, z]),
            (entering_hbm, entering_ref), (arriving_hbm, arriving_ref), (gain_hbm, gain_ref),
            (live_hbm, live_ref), (blocks_hbm, blocks_ref), (count_hbm, count_ref), (owner_hbm, owner_ref),
        ))
    ]
    for copy in inputs:
        copy.start()
    weights_up.start()
    weights_down.start()
    for copy in inputs:
        copy.wait()
    recv_buf[dp] = jnp.zeros(recv_buf.shape[1:], BF16)

    pl.semaphore_wait(barrier, (nd - 1) + (nt - 1) + 2 * nz)

    def together(ref, sends, receives):
        return remote(ref, ref, sends, receives, partner)

    def gather_start(g, src, dst, target_section, count):
        def send(k):
            j = far_first(k)
            remote(
                src, dst.at[core, z], gather_send.at[g, 0], gather_recv.at[g, 0],
                (target_section, zup(j) * 2 + core, tensor),
            ).start()
        loop(0, count, send)
        all_of = together(dst.at[0, :count], gather_send.at[g, 0], gather_recv.at[g, 0])
        leaving.append(all_of.wait_send)
        coming["gather", g] = all_of.wait_recv

    def relay(g, dst):
        coming.pop(("gather", g))()
        half = together(dst.at[core], gather_send.at[g, 1], gather_recv.at[g, 1])
        half.start()
        leaving.append(half.wait_send)
        coming["relay", g] = half.wait_recv

    def gather_wait(g):
        coming.pop(("relay", g))()

    def both_start(g, src, dst, target_section):
        def send(k):
            j = far_first(k)
            for other_core in range(2):
                remote(
                    src, dst.at[core, z], gather_send.at[g, 0], gather_recv.at[g, 0],
                    (target_section, zup(j) * 2 + lax.rem(core + other_core, 2), tensor),
                ).start()
        loop(0, nz, send)
        all_of = together(dst, gather_send.at[g, 0], gather_recv.at[g, 0])
        leaving.append(all_of.wait_send)
        coming["both", g] = all_of.wait_recv

    def both_wait(g):
        coming.pop(("both", g))()

    mine = pl.ds(pl.multiple_of(tensor * part, part), part)

    def sum_start(g, sent, got):
        for j in range(1, nt):
            remote(
                sent.at[pl.ds(pl.multiple_of(tup(j) * part, part), part)], got.at[j],
                tensor_send.at[g], tensor_recv.at[g], (section, dp, tup(j)),
            ).start()
        all_of = together(got.at[1:nt], tensor_send.at[g], tensor_recv.at[g])
        leaving.append(all_of.wait_send)
        coming["sum", g] = all_of.wait_recv

    def sum_end(g, sent, got):
        coming.pop(("sum", g))()
        total = sent[mine].astype(F32)
        for j in range(1, nt):
            total = total + got[j].astype(F32)
        return total

    def share_start(g, mix):
        for j in range(1, nt):
            remote(
                mix.at[mine], mix.at[mine], tensor_send.at[g], tensor_recv.at[g], (section, dp, tup(j))
            ).start()
        all_of = together(mix.at[: (nt - 1) * part], tensor_send.at[g], tensor_recv.at[g])
        leaving.append(all_of.wait_send)
        coming["share", g] = all_of.wait_recv

    def share_wait(g):
        coming.pop(("share", g))()

    def reduce_start(g, value, keep, half, other):
        keep[...] = value.reshape(2, rows // 2, width)
        half[...] = keep[1 - core].astype(BF16)
        swap = remote(half, other, reduce_send.at[g, 0], reduce_recv.at[g, 0], partner)
        swap.start()
        leaving.append(swap.wait_send)
        coming["swap", g] = swap.wait_recv

    def reduce_middle(g, keep, other, chip, got):
        coming.pop(("swap", g))()
        total = keep[core] + other[...].astype(F32)
        chip[...] = total.reshape(nz, local, width).astype(BF16)
        got[z] = chip[z]

        def send(k):
            j = far_first(k)
            remote(
                chip.at[zup(j)], got.at[z], reduce_send.at[g, 1], reduce_recv.at[g, 1],
                (section, zup(j) * 2 + core, tensor),
            ).start()
        loop(0, nz - 1, send)
        all_of = together(got.at[: nz - 1], reduce_send.at[g, 1], reduce_recv.at[g, 1])
        leaving.append(all_of.wait_send)
        coming["reduce", g] = all_of.wait_recv

    def reduce_end(g, got):
        coming.pop(("reduce", g))()
        return jnp.sum(got[...].astype(F32), axis=0)

    def scatter_start(g, value, parts, got):
        parts[...] = value.reshape(parts.shape).astype(BF16)
        got[dp] = parts[core, z]

        def send(j, other_core):
            target = lax.rem(core + other_core, 2)
            remote(
                parts.at[target, zup(j)], got.at[dp], reduce_send.at[g, 0], reduce_recv.at[g, 0],
                (section, zup(j) * 2 + target, tensor),
            ).start()

        def send_both(k):
            send(far_first(k), 0)
            send(far_first(k), 1)
        loop(0, nz - 1, send_both)
        send(0, 1)
        all_of = together(got.at[: nd - 1], reduce_send.at[g, 0], reduce_recv.at[g, 0])
        leaving.append(all_of.wait_send)
        coming["scatter", g] = all_of.wait_recv

    def scatter_end(g, got):
        coming.pop(("scatter", g))()
        return jnp.sum(got[...].astype(F32), axis=0)

    def flat_rows(ref):
        return ref[...].astype(F32).reshape(rows, width)

    gain = gain_ref[...].astype(F32)

    def scales_of(lane_squares):
        return lax.rsqrt(jnp.sum(lane_squares, axis=1, keepdims=True) / dw + EPSILON)

    def up_product(widened):
        normed = (widened * gain).astype(BF16)
        product = jnp.dot(normed, up_ref[...], preferred_element_type=F32)
        return normed, product.astype(BF16), lane_blocks_sum(widened * widened).astype(BF16)

    def to_table(table, first, turn, value):
        for b in range(value.shape[1] // BLK):
            table[first + b, turn * rows : (turn + 1) * rows, :] = value[:, b * BLK : (b + 1) * BLK]

    hidden_blocks = hidden // BLK
    channel_blocks = width // BLK

    def backward_middle(total_p, total_a, mix):
        product, scales = total_p
        inner = product * scales
        gate = jax.nn.sigmoid(inner)
        hidden_grad = total_a * gate * (1.0 + inner * (1.0 - gate))
        mix[mine, :hidden] = (hidden_grad * scales).astype(BF16)
        per_lane = lane_blocks_sum(hidden_grad * product)
        mix[mine, hidden:] = (per_lane * (scales * scales * scales / dw)).astype(BF16)

    def activated_of(product, scales):
        inner = product * scales
        return (inner * jax.nn.sigmoid(inner)).astype(BF16)

    def product_end(g, sent, got):
        total = sum_end(g, sent, got)
        return total[:, :hidden], scales_of(total[:, hidden:])

    def normed_grad(mix, widened):
        part_sum = times_transposed(mix[:, :hidden], up_ref[...])
        coefficient = jnp.sum(mix[:, hidden:].astype(F32), axis=1, keepdims=True)
        return part_sum * gain - coefficient * widened

    def stored_product(ref, product, lane_squares):
        ref[:, :hidden] = product
        ref[:, hidden:] = lane_squares

    def rows_of(ref, which):
        return ref[:, :, which].astype(F32).reshape(rows, width)

    gather_start(0, all_a.at[core, z], all_a, section, nz - 1)
    capacity = owner_ref.shape[0]
    up_count = hidden_blocks * channel_blocks
    left_index, right_index = [], []
    for k in range(capacity):
        number = blocks_ref[k, 0, dp]
        down_number = jnp.maximum(number - up_count, 0)
        is_up = number < up_count
        left_index.append(
            jnp.where(is_up, number // hidden_blocks, channel_blocks + down_number // channel_blocks)
        )
        right_index.append(
            jnp.where(is_up, number % hidden_blocks, hidden_blocks + down_number % channel_blocks)
        )
    my_count = count_ref[dp]
    my_owners = [owner_ref[k, 0, dp] for k in range(capacity)]
    picks = []
    for o in range(nd):
        pick = jnp.int32(0)
        for k in range(capacity):
            pick = jnp.where((my_owners[k] == o) & (k < my_count), k, pick)
        picks.append(pick)
    taken = jnp.int32(0)
    sources = [jnp.int32(0) for _ in range(capacity)]
    for h in range(nd):
        sends = jnp.int32(0)
        for k in range(capacity):
            sends = jnp.where((owner_ref[k, 0, h] == dp) & (k < count_ref[h]), 1, sends)
        for i in range(capacity):
            sources[i] = jnp.where((sends == 1) & (taken == i), h, sources[i])
        taken = taken + sends

    relay(0, all_a)
    gather_start(1, all_s.at[core, z], all_s, section, nz - 1)
    gather_start(4, all_x.at[core, z], all_x, section, nz - 1)
    weights_up.wait()
    gather_wait(0)
    normed0, *made = up_product(rows_of(all_a, 0))
    stored_product(sent_p0, *made)
    sum_start(0, sent_p0, got_p0)
    weights_down.wait()
    dy0 = rows_of(all_a, 1).astype(BF16)
    sent_a0[...] = times_transposed(dy0, down_ref[...]).astype(BF16)
    sum_start(1, sent_a0, got_a0)
    to_table(left_table, 0, 0, normed0)
    to_table(right_table, hidden_blocks, 0, dy0)

    relay(1, all_s)
    gather_wait(1)
    _, *made = up_product(flat_rows(all_s))
    stored_product(sent_f0, *made)

    total_p0 = product_end(0, sent_p0, got_p0)
    total_a0 = sum_end(1, sent_a0, got_a0)
    backward_middle(total_p0, total_a0, mix_s0)
    share_start(6, mix_s0)
    sum_start(2, sent_f0, got_f0)
    mix_h0[mine] = activated_of(*total_p0)

    relay(4, all_x)
    gather_wait(4)
    normed1, *made = up_product(flat_rows(all_x))
    stored_product(sent_p1, *made)
    to_table(left_table, 0, 1, normed1)

    share_wait(6)
    scatter_start(0, normed_grad(mix_s0, rows_of(all_a, 0)), parts_b0, rows_b0)
    sum_start(3, sent_p1, got_p1)
    to_table(right_table, 0, 0, mix_s0[:, :hidden])
    total_f0 = product_end(2, sent_f0, got_f0)
    mix_f0[mine] = activated_of(*total_f0)
    share_start(7, mix_f0)
    share_start(8, mix_h0)

    row_ids = dp * local + lax.broadcasted_iota(jnp.int32, (local, width), 0)
    masked = jnp.where(row_ids < live_ref[0], arriving_ref[...].astype(F32), 0.0)
    input_grad0 = all_a[core, z, 1].astype(F32) + scatter_end(0, rows_b0)
    src_d[...] = jnp.where(section == 0, masked, input_grad0).astype(BF16)
    both_start(2, src_d, all_d, before)
    grads_ref[0] = input_grad0.astype(BF16)

    total_p1, scales1 = product_end(3, sent_p1, got_p1)
    held_p1[...] = total_p1
    held_scale1[...] = jnp.broadcast_to(scales1, held_scale1.shape)
    mix_h1[mine] = activated_of(total_p1, scales1)
    share_start(9, mix_h1)
    share_wait(7)
    reduce_start(1, jnp.dot(mix_f0[...], down_ref[...], preferred_element_type=F32), keep_f0, half_f0, other_f0)
    reduce_middle(1, keep_f0, other_f0, chip_f0, rows_f0)
    share_wait(8)
    to_table(left_table, channel_blocks, 0, mix_h0[...])

    both_wait(2)
    dy1 = flat_rows(all_d).astype(BF16)
    sent_a1[...] = times_transposed(dy1, down_ref[...]).astype(BF16)
    sum_start(4, sent_a1, got_a1)
    to_table(right_table, hidden_blocks, 1, dy1)
    share_wait(9)
    to_table(left_table, channel_blocks, 1, mix_h1[...])

    output0 = all_s[core, z].astype(F32) + reduce_end(1, rows_f0)
    src_f[...] = jnp.where(section == ns - 1, entering_ref[...].astype(F32), output0).astype(BF16)
    both_start(3, src_f, all_f, after)
    outputs_ref[0] = output0.astype(BF16)

    total_a1 = sum_end(4, sent_a1, got_a1)
    backward_middle((held_p1[...], held_scale1[:, :1]), total_a1, mix_s1)
    share_start(10, mix_s1)

    share_wait(10)
    to_table(right_table, 0, 1, mix_s1[:, :hidden])
    for k in range(capacity):
        block = lax.dot_general(
            left_table[left_index[k]], right_table[right_index[k]],
            (((0,), (0,)), ((), ())), preferred_element_type=F32,
        )
        block_buf[k] = block.astype(BF16)
    for o in range(nd):
        send_buf[o] = block_buf[picks[o]]

    def send_block(k):
        owner = lax.rem(dp + nz + (1 - 2 * (k % 2)) * ((k + 1) // 2), nd)
        remote(
            send_buf.at[owner], recv_buf.at[dp], block_send.at[0], block_recv.at[0],
            (section, owner, tensor),
        ).start()
    loop(0, nd - 1, send_block)
    all_blocks = together(recv_buf.at[: nd - 1], block_send.at[0], block_recv.at[0])
    leaving.append(all_blocks.wait_send)
    coming["blocks", 0] = all_blocks.wait_recv

    both_wait(3)
    _, *made = up_product(flat_rows(all_f))
    stored_product(sent_f1, *made)
    sum_start(5, sent_f1, got_f1)

    reduce_start(2, normed_grad(mix_s1, flat_rows(all_x)), keep_b1, half_b1, other_b1)
    reduce_middle(2, keep_b1, other_b1, chip_b1, rows_b1)

    total_f1 = product_end(5, sent_f1, got_f1)
    mix_f1[mine] = activated_of(*total_f1)
    share_start(11, mix_f1)
    share_wait(11)
    reduce_start(3, jnp.dot(mix_f1[...], down_ref[...], preferred_element_type=F32), keep_f1, half_f1, other_f1)
    reduce_middle(3, keep_f1, other_f1, chip_f1, rows_f1)
    grads_ref[1] = (all_d[core, z].astype(F32) + reduce_end(2, rows_b1)).astype(BF16)
    outputs_ref[1] = (all_f[core, z].astype(F32) + reduce_end(3, rows_f1)).astype(BF16)

    coming.pop(("blocks", 0))()
    for i in range(capacity):
        owned_ref[i] = jnp.where(i < taken, recv_buf[sources[i]].astype(F32), 0.0).astype(BF16)
        filled_ref[i] = jnp.where(i < taken, jnp.ones((1, LANES), F32), 0.0)

    for wait in leaving:
        wait()


def adam(
    outputs_in, grads_in, owned_ref, filled_ref, first_ref, second_ref,
    outputs_ref, grads_ref, first_out, second_out, direction_out,
):
    outputs_ref[...] = outputs_in[...]
    grads_ref[...] = grads_in[...]
    for i in range(owned_ref.shape[0]):
        grad = owned_ref[i].astype(F32)
        filled = filled_ref[i] > 0.5
        first = 0.9 * first_ref[i] + 0.1 * grad
        second = 0.999 * second_ref[i] + 0.001 * grad * grad
        first_out[i] = jnp.where(filled, first, 0.0)
        second_out[i] = jnp.where(filled, second, 0.0)
        direction_out[i] = jnp.where(filled, first / (jnp.sqrt(second) + 1e-08), 0.0)


def by_slot(lists):
    return jnp.transpose(lists, (0, 3, 1, 2))[0]


def body(
    sizes,
    section_inputs, entering, grad_outputs, arriving, live_rows, stashed_inputs, norm_gain,
    up_weight, down_weight, held_blocks, held_count, held_owner, first_moment, second_moment,
):
    ns, nz, nt = sizes
    nd = 2 * nz
    local, width = section_inputs.shape[1:]
    hidden = up_weight.shape[2]
    rows = local * nd
    part = rows // nt
    capacity = held_owner.shape[3]
    turns = stashed_inputs.shape[1]
    blocks = hidden // BLK + width // BLK
    vmem = pl.BlockSpec(memory_space=pltpu.VMEM)
    anywhere = pl.BlockSpec(memory_space=pl.ANY)
    wide = hidden + LANES

    def several(count, shape, dtype):
        return [pltpu.VMEM(shape, dtype) for _ in range(count)]

    scratch = [
        pltpu.VMEM((width, hidden), BF16), pltpu.VMEM((hidden, width), BF16),
        pltpu.SMEM((1,), jnp.int32), pltpu.SMEM((capacity, 1, nd), jnp.int32),
        pltpu.SMEM((nd,), jnp.int32), pltpu.SMEM((capacity, 1, nd), jnp.int32),
        *several(2, (local, width), BF16), pltpu.VMEM((1, width), BF16),
        *several(2, (local, width), BF16),
        pltpu.VMEM((2, nz, 2, local, width), BF16),
        *several(4, (2, nz, local, width), BF16),
        *[pltpu.VMEM((rows, w), BF16) for w in (wide, hidden, wide, wide, hidden, wide)],
        *[pltpu.VMEM((nt, part, w), BF16) for w in (wide, hidden, wide, wide, hidden, wide)],
        *[pltpu.VMEM((rows, w), BF16) for w in (wide, hidden, hidden, hidden, wide, hidden)],
        *several(3, (2, rows // 2, width), F32),
        *several(3, (rows // 2, width), BF16),
        *several(3, (rows // 2, width), BF16),
        *several(3, (nz, local, width), BF16),
        *several(3, (nz, local, width), BF16),
        pltpu.VMEM((2, nz, local, width), BF16), pltpu.VMEM((nd, local, width), BF16),
        *several(2, (blocks, turns * rows, BLK), BF16),
        pltpu.VMEM((capacity, BLK, BLK), BF16),
        *several(2, (nd, BLK, BLK), BF16),
        pltpu.VMEM((part, hidden), F32), pltpu.VMEM((part, LANES), F32),
        pltpu.SemaphoreType.DMA((2,)), pltpu.SemaphoreType.DMA((11,)),
        pltpu.SemaphoreType.DMA((5, 2)), pltpu.SemaphoreType.DMA((5, 2)),
        pltpu.SemaphoreType.DMA((12,)), pltpu.SemaphoreType.DMA((12,)),
        pltpu.SemaphoreType.DMA((4, 2)), pltpu.SemaphoreType.DMA((4, 2)),
        pltpu.SemaphoreType.DMA((1,)), pltpu.SemaphoreType.DMA((1,)),
    ]
    outputs, grads, owned, filled = pl.pallas_call(
        functools.partial(kernel, sizes),
        out_shape=(
            jax.ShapeDtypeStruct((turns, local, width), BF16),
            jax.ShapeDtypeStruct((turns, local, width), BF16),
            jax.ShapeDtypeStruct((capacity, BLK, BLK), BF16),
            jax.ShapeDtypeStruct((capacity, 1, LANES), F32),
        ),
        in_specs=[anywhere] * 12,
        out_specs=[vmem] * 4,
        scratch_shapes=scratch,
        compiler_params=pltpu.CompilerParams(
            collective_id=0, has_side_effects=True, vmem_limit_bytes=56 * 1024 * 1024
        ),
        name="relay",
    )(
        live_rows, by_slot(held_blocks), held_count[0, 0], by_slot(held_owner),
        section_inputs[0], entering[0], grad_outputs[0], arriving[0], stashed_inputs[0], norm_gain,
        up_weight[0], down_weight[0],
    )
    block_shape = jax.ShapeDtypeStruct((capacity, BLK, BLK), F32)
    outputs, grads, first_out, second_out, direction_out = pl.pallas_call(
        adam,
        out_shape=(
            jax.ShapeDtypeStruct(outputs.shape, BF16), jax.ShapeDtypeStruct(grads.shape, BF16),
            block_shape, block_shape, block_shape,
        ),
        in_specs=[vmem] * 6,
        out_specs=[vmem] * 5,
        name="adam",
    )(outputs, grads, owned, filled, first_moment[0, 0, 0], second_moment[0, 0, 0])
    return (
        outputs[None], grads[None],
        first_out[None, None, None], second_out[None, None, None], direction_out[None, None, None],
    )


def solution(mesh):
    sizes = (mesh.shape["section"], mesh.shape["dp"] // 2, mesh.shape["tensor"])
    return jax.shard_map(
        functools.partial(body, sizes),
        mesh=mesh,
        in_specs=(
            P("section", "dp", "tensor"),
            P(None, "dp", "tensor"),
            P("section", "dp", "tensor"),
            P(None, "dp", "tensor"),
            P(),
            P("section", None, "dp", "tensor"),
            P("section", "tensor"),
            P("section", "tensor", "dp"),
            P("section", "dp", "tensor"),
            P("section", "tensor", None, None),
            P("section", "tensor", None),
            P("section", "tensor", None, None),
            P("section", "tensor", "dp", None, None, None),
            P("section", "tensor", "dp", None, None, None),
        ),
        out_specs=(
            P("section", None, "dp", "tensor"),
            P("section", None, "dp", "tensor"),
            P("section", "tensor", "dp", None, None, None),
            P("section", "tensor", "dp", None, None, None),
            P("section", "tensor", "dp", None, None, None),
        ),
        check_vma=False,
    )
```

```python
import functools

import jax
import jax.numpy as jnp
from jax import lax
from jax.experimental import pallas as pl
from jax.experimental.pallas import tpu as pltpu
from jax.sharding import PartitionSpec as P

MESH = pl.DeviceIdType.MESH
BLK = 128
LANES = 128
EPSILON = 1e-06
F32 = jnp.float32
BF16 = jnp.bfloat16


def times_transposed(left, right):
    return lax.dot_general(left, right, (((1,), (1,)), ((), ())), preferred_element_type=F32)


def lane_blocks_sum(value):
    total = value[:, :LANES]
    for start in range(LANES, value.shape[1], LANES):
        total = total + value[:, start : start + LANES]
    return total


def kernel(
    sizes,
    live_hbm, blocks_hbm, count_hbm, owner_hbm,
    section_hbm, entering_hbm, grad_hbm, arriving_hbm, stash_hbm, gain_hbm,
    up_hbm, down_hbm,
    outputs_ref, grads_ref, owned_ref, filled_ref,
    up_ref, down_ref,
    live_ref, blocks_ref, count_ref, owner_ref,
    entering_ref, arriving_ref, gain_ref,
    src_f, src_d,
    all_a, all_s, all_x, all_f, all_d,
    sent_p0, sent_a0, sent_f0, sent_p1, sent_a1, sent_f1,
    got_p0, got_a0, got_f0, got_p1, got_a1, got_f1,
    mix_s0, mix_h0, mix_f0, mix_h1, mix_s1, mix_f1,
    keep_f0, keep_b1, keep_f1,
    half_f0, half_b1, half_f1,
    other_f0, other_b1, other_f1,
    chip_f0, chip_b1, chip_f1,
    rows_f0, rows_b1, rows_f1,
    parts_b0, rows_b0,
    left_table, right_table, block_buf, send_buf, recv_buf,
    held_p1, held_scale1,
    weight_sem, input_sem,
    gather_send, gather_recv,
    tensor_send, tensor_recv,
    reduce_send, reduce_recv,
    block_send, block_recv,
):
    ns, nz, nt = sizes
    nd = 2 * nz
    local, width = entering_ref.shape
    hidden = up_ref.shape[1]
    rows = local * nd
    part = rows // nt
    dw = width * nt
    section = lax.axis_index("section")
    dp = lax.axis_index("dp")
    tensor = lax.axis_index("tensor")
    z = dp // 2
    core = dp % 2
    partner = (section, z * 2 + 1 - core, tensor)
    after = lax.rem(section + 1, ns)
    before = lax.rem(section + ns - 1, ns)

    leaving = []
    coming = {}

    def remote(src, dst, send_sem, recv_sem, device):
        return pltpu.make_async_remote_copy(
            src_ref=src, dst_ref=dst, send_sem=send_sem, recv_sem=recv_sem,
            device_id=device, device_id_type=MESH,
        )

    def far_first(k):
        return nz // 2 + (1 - 2 * (k % 2)) * ((k + 1) // 2)

    def zup(j):
        return lax.rem(z + j, nz)

    def zdown(j):
        return lax.rem(z + nz - j, nz)

    def tup(j):
        return lax.rem(tensor + j, nt)

    def loop(lo, hi, fn):
        def step(k, carry):
            fn(k)
            return carry
        lax.fori_loop(lo, hi, step, 0)

    weights_up = pltpu.make_async_copy(up_hbm, up_ref, weight_sem.at[0])
    weights_down = pltpu.make_async_copy(down_hbm, down_ref, weight_sem.at[1])

    barrier = pltpu.get_barrier_semaphore()

    def greet(device):
        pl.semaphore_signal(barrier, inc=1, device_id=device, device_id_type=MESH)

    def greet_z(k):
        greet((section, zup(far_first(k)) * 2 + core, tensor))

    loop(0, nz - 1, greet_z)
    greet(partner)
    for j in range(1, nt):
        greet((section, dp, tup(j)))
    greet((after, dp, tensor))
    greet((before, dp, tensor))

    inputs = [
        pltpu.make_async_copy(src, dst, input_sem.at[i])
        for i, (src, dst) in enumerate((
            (stash_hbm.at[0], all_a.at[core, z, 0]), (grad_hbm, all_a.at[core, z, 1]),
            (section_hbm, all_s.at[core, z]), (stash_hbm.at[1], all_x.at[core, z]),
            (entering_hbm, entering_ref), (arriving_hbm, arriving_ref), (gain_hbm, gain_ref),
            (live_hbm, live_ref), (blocks_hbm, blocks_ref), (count_hbm, count_ref), (owner_hbm, owner_ref),
        ))
    ]
    for copy in inputs:
        copy.start()
    weights_up.start()
    weights_down.start()
    for copy in inputs:
        copy.wait()
    recv_buf[dp] = jnp.zeros(recv_buf.shape[1:], BF16)

    pl.semaphore_wait(barrier, nz + (nt - 1) + 2)

    def together(ref, sends, receives):
        return remote(ref, ref, sends, receives, partner)

    def gather_start(g, src, dst, target_section, count):
        def send(k):
            j = far_first(k)
            remote(
                src, dst.at[core, z], gather_send.at[g, 0], gather_recv.at[g, 0],
                (target_section, zup(j) * 2 + core, tensor),
            ).start()
        loop(0, count, send)
        all_of = together(dst.at[0, :count], gather_send.at[g, 0], gather_recv.at[g, 0])
        leaving.append(all_of.wait_send)
        coming["gather", g] = all_of.wait_recv

    def relay(g, dst):
        coming.pop(("gather", g))()
        half = together(dst.at[core], gather_send.at[g, 1], gather_recv.at[g, 1])
        half.start()
        leaving.append(half.wait_send)
        coming["relay", g] = half.wait_recv

    def gather_wait(g):
        coming.pop(("relay", g))()

    def both_start(g, src, dst, target_section):
        def send(k):
            j = far_first(k)
            for other_core in range(2):
                remote(
                    src, dst.at[core, z], gather_send.at[g, 0], gather_recv.at[g, 0],
                    (target_section, zup(j) * 2 + lax.rem(core + other_core, 2), tensor),
                ).start()
        loop(0, nz, send)
        all_of = together(dst, gather_send.at[g, 0], gather_recv.at[g, 0])
        leaving.append(all_of.wait_send)
        coming["both", g] = all_of.wait_recv

    def both_wait(g):
        coming.pop(("both", g))()

    mine = pl.ds(pl.multiple_of(tensor * part, part), part)

    def sum_start(g, sent, got, columns=slice(None)):
        for j in range(1, nt):
            remote(
                sent.at[pl.ds(pl.multiple_of(tup(j) * part, part), part), columns], got.at[j, :, columns],
                tensor_send.at[g], tensor_recv.at[g], (section, dp, tup(j)),
            ).start()
        all_of = together(got.at[1:nt, :, columns], tensor_send.at[g], tensor_recv.at[g])
        leaving.append(all_of.wait_send)
        coming["sum", g] = all_of.wait_recv

    def sum_end(g, sent, got, columns=slice(None)):
        coming.pop(("sum", g))()
        total = sent[mine, columns].astype(F32)
        for j in range(1, nt):
            total = total + got[j, :, columns].astype(F32)
        return total

    def share_start(g, mix, columns=slice(None)):
        for j in range(1, nt):
            remote(
                mix.at[mine, columns], mix.at[mine, columns],
                tensor_send.at[g], tensor_recv.at[g], (section, dp, tup(j)),
            ).start()
        all_of = together(mix.at[: (nt - 1) * part, columns], tensor_send.at[g], tensor_recv.at[g])
        leaving.append(all_of.wait_send)
        coming["share", g] = all_of.wait_recv

    def share_wait(g):
        coming.pop(("share", g))()

    def reduce_start(g, value, keep, half, other):
        keep[...] = value.reshape(2, rows // 2, width)
        half[...] = keep[1 - core].astype(BF16)
        swap = remote(half, other, reduce_send.at[g, 0], reduce_recv.at[g, 0], partner)
        swap.start()
        leaving.append(swap.wait_send)
        coming["swap", g] = swap.wait_recv

    def reduce_middle(g, keep, other, chip, got):
        coming.pop(("swap", g))()
        total = keep[core] + other[...].astype(F32)
        chip[...] = total.reshape(nz, local, width).astype(BF16)
        got[z] = chip[z]

        def send(k):
            j = far_first(k)
            remote(
                chip.at[zup(j)], got.at[z], reduce_send.at[g, 1], reduce_recv.at[g, 1],
                (section, zup(j) * 2 + core, tensor),
            ).start()
        loop(0, nz - 1, send)
        all_of = together(got.at[: nz - 1], reduce_send.at[g, 1], reduce_recv.at[g, 1])
        leaving.append(all_of.wait_send)
        coming["reduce", g] = all_of.wait_recv

    def reduce_end(g, got):
        coming.pop(("reduce", g))()
        return jnp.sum(got[...].astype(F32), axis=0)

    def scatter_start(g, value, parts, got):
        parts[...] = value.reshape(parts.shape).astype(BF16)
        got[dp] = parts[core, z]

        def send(j, other_core):
            target = lax.rem(core + other_core, 2)
            remote(
                parts.at[target, zup(j)], got.at[dp], reduce_send.at[g, 0], reduce_recv.at[g, 0],
                (section, zup(j) * 2 + target, tensor),
            ).start()

        def send_both(k):
            send(far_first(k), 0)
            send(far_first(k), 1)
        loop(0, nz - 1, send_both)
        send(0, 1)
        all_of = together(got.at[: nd - 1], reduce_send.at[g, 0], reduce_recv.at[g, 0])
        leaving.append(all_of.wait_send)
        coming["scatter", g] = all_of.wait_recv

    def scatter_end(g, got):
        coming.pop(("scatter", g))()
        return jnp.sum(got[...].astype(F32), axis=0)

    def flat_rows(ref):
        return ref[...].astype(F32).reshape(rows, width)

    gain = gain_ref[...].astype(F32)

    def scales_of(lane_squares):
        return lax.rsqrt(jnp.sum(lane_squares, axis=1, keepdims=True) / dw + EPSILON)

    cut = hidden // LANES // 2 * LANES
    hidden_parts = (slice(0, cut), slice(cut, hidden))
    product_parts = (slice(0, LANES + cut), slice(LANES + cut, LANES + hidden))
    mix_parts = (slice(0, cut), slice(cut, hidden + LANES))

    def normed_of(widened, sent):
        sent[:, :LANES] = lane_blocks_sum(widened * widened).astype(BF16)
        return (widened * gain).astype(BF16)

    def product_of(normed, sent):
        sent[:, LANES:] = jnp.dot(normed, up_ref[...], preferred_element_type=F32).astype(BF16)

    def product_part(normed, sent, i):
        columns = hidden_parts[i]
        product = jnp.dot(normed, up_ref[:, columns], preferred_element_type=F32)
        sent[:, LANES + columns.start : LANES + columns.stop] = product.astype(BF16)

    def act_grad_part(grads, sent, i):
        columns = hidden_parts[i]
        sent[:, columns] = times_transposed(grads, down_ref[columns, :]).astype(BF16)

    def to_table(table, first, turn, value):
        for b in range(value.shape[1] // BLK):
            table[first + b, turn * rows : (turn + 1) * rows, :] = value[:, b * BLK : (b + 1) * BLK]

    hidden_blocks = hidden // BLK
    channel_blocks = width // BLK

    def backward_part(product, scales, act_grad, mix, i):
        inner = product * scales
        gate = jax.nn.sigmoid(inner)
        hidden_grad = act_grad * gate * (1.0 + inner * (1.0 - gate))
        mix[mine, hidden_parts[i]] = (hidden_grad * scales).astype(BF16)
        return lane_blocks_sum(hidden_grad * product)

    def scale_part(per_lane, scales, mix):
        mix[mine, hidden:] = (per_lane * (scales * scales * scales / dw)).astype(BF16)

    def activated_of(product, scales):
        inner = product * scales
        return (inner * jax.nn.sigmoid(inner)).astype(BF16)

    def product_end(g, sent, got):
        total = sum_end(g, sent, got)
        return total[:, LANES:], scales_of(total[:, :LANES])

    def normed_grad_part(mix, i):
        columns = hidden_parts[i]
        return times_transposed(mix[:, columns], up_ref[:, columns])

    def row_grads(part_sum, mix, widened):
        coefficient = jnp.sum(mix[:, hidden:].astype(F32), axis=1, keepdims=True)
        return part_sum * gain - coefficient * widened

    def rows_of(ref, which):
        return ref[:, :, which].astype(F32).reshape(rows, width)

    gather_start(0, all_a.at[core, z], all_a, section, nz - 1)
    capacity = owner_ref.shape[0]
    up_count = hidden_blocks * channel_blocks
    left_index, right_index = [], []
    for k in range(capacity):
        number = blocks_ref[k, 0, dp]
        down_number = jnp.maximum(number - up_count, 0)
        is_up = number < up_count
        left_index.append(
            jnp.where(is_up, number // hidden_blocks, channel_blocks + down_number // channel_blocks)
        )
        right_index.append(
            jnp.where(is_up, number % hidden_blocks, hidden_blocks + down_number % channel_blocks)
        )
    my_count = count_ref[dp]
    my_owners = [owner_ref[k, 0, dp] for k in range(capacity)]
    picks = []
    for o in range(nd):
        pick = jnp.int32(0)
        for k in range(capacity):
            pick = jnp.where((my_owners[k] == o) & (k < my_count), k, pick)
        picks.append(pick)
    taken = jnp.int32(0)
    sources = [jnp.int32(0) for _ in range(capacity)]
    for h in range(nd):
        sends = jnp.int32(0)
        for k in range(capacity):
            sends = jnp.where((owner_ref[k, 0, h] == dp) & (k < count_ref[h]), 1, sends)
        for i in range(capacity):
            sources[i] = jnp.where((sends == 1) & (taken == i), h, sources[i])
        taken = taken + sends

    relay(0, all_a)
    gather_start(1, all_s.at[core, z], all_s, section, nz - 1)
    gather_start(4, all_x.at[core, z], all_x, section, nz - 1)
    weights_up.wait()
    gather_wait(0)
    normed0 = normed_of(rows_of(all_a, 0), sent_p0)
    product_part(normed0, sent_p0, 0)
    sum_start(0, sent_p0, got_p0, product_parts[0])
    weights_down.wait()
    dy0 = rows_of(all_a, 1).astype(BF16)
    act_grad_part(dy0, sent_a0, 0)
    sum_start(1, sent_a0, got_a0, hidden_parts[0])
    product_part(normed0, sent_p0, 1)
    sum_start(12, sent_p0, got_p0, product_parts[1])
    act_grad_part(dy0, sent_a0, 1)
    sum_start(13, sent_a0, got_a0, hidden_parts[1])
    to_table(left_table, 0, 0, normed0)
    to_table(right_table, hidden_blocks, 0, dy0)

    relay(1, all_s)
    gather_wait(1)
    product_of(normed_of(flat_rows(all_s), sent_f0), sent_f0)

    total_p0 = sum_end(0, sent_p0, got_p0, product_parts[0])
    scales0 = scales_of(total_p0[:, :LANES])
    first_p0 = total_p0[:, LANES:]
    total_a0 = sum_end(1, sent_a0, got_a0, hidden_parts[0])
    per_lane = backward_part(first_p0, scales0, total_a0, mix_s0, 0)
    share_start(6, mix_s0, mix_parts[0])
    last_p0 = sum_end(12, sent_p0, got_p0, product_parts[1])
    total_a0 = sum_end(13, sent_a0, got_a0, hidden_parts[1])
    scale_part(per_lane + backward_part(last_p0, scales0, total_a0, mix_s0, 1), scales0, mix_s0)
    share_start(14, mix_s0, mix_parts[1])
    sum_start(2, sent_f0, got_f0)
    mix_h0[mine, hidden_parts[0]] = activated_of(first_p0, scales0)
    mix_h0[mine, hidden_parts[1]] = activated_of(last_p0, scales0)

    relay(4, all_x)
    gather_wait(4)
    normed1 = normed_of(flat_rows(all_x), sent_p1)
    product_of(normed1, sent_p1)
    to_table(left_table, 0, 1, normed1)

    share_wait(6)
    part_sum = normed_grad_part(mix_s0, 0)
    share_wait(14)
    part_sum = part_sum + normed_grad_part(mix_s0, 1)
    scatter_start(0, row_grads(part_sum, mix_s0, rows_of(all_a, 0)), parts_b0, rows_b0)
    sum_start(3, sent_p1, got_p1)
    to_table(right_table, 0, 0, mix_s0[:, :hidden])
    total_f0 = product_end(2, sent_f0, got_f0)
    mix_f0[mine] = activated_of(*total_f0)
    share_start(7, mix_f0)
    share_start(8, mix_h0)

    row_ids = dp * local + lax.broadcasted_iota(jnp.int32, (local, width), 0)
    masked = jnp.where(row_ids < live_ref[0], arriving_ref[...].astype(F32), 0.0)
    input_grad0 = all_a[core, z, 1].astype(F32) + scatter_end(0, rows_b0)
    src_d[...] = jnp.where(section == 0, masked, input_grad0).astype(BF16)
    both_start(2, src_d, all_d, before)
    grads_ref[0] = input_grad0.astype(BF16)

    total_p1, scales1 = product_end(3, sent_p1, got_p1)
    held_p1[...] = total_p1
    held_scale1[...] = jnp.broadcast_to(scales1, held_scale1.shape)
    mix_h1[mine] = activated_of(total_p1, scales1)
    share_start(9, mix_h1)
    share_wait(7)
    reduce_start(1, jnp.dot(mix_f0[...], down_ref[...], preferred_element_type=F32), keep_f0, half_f0, other_f0)
    reduce_middle(1, keep_f0, other_f0, chip_f0, rows_f0)
    share_wait(8)
    to_table(left_table, channel_blocks, 0, mix_h0[...])

    both_wait(2)
    dy1 = flat_rows(all_d).astype(BF16)
    act_grad_part(dy1, sent_a1, 0)
    sum_start(4, sent_a1, got_a1, hidden_parts[0])
    act_grad_part(dy1, sent_a1, 1)
    sum_start(15, sent_a1, got_a1, hidden_parts[1])
    to_table(right_table, hidden_blocks, 1, dy1)
    share_wait(9)
    to_table(left_table, channel_blocks, 1, mix_h1[...])

    output0 = all_s[core, z].astype(F32) + reduce_end(1, rows_f0)
    src_f[...] = jnp.where(section == ns - 1, entering_ref[...].astype(F32), output0).astype(BF16)
    both_start(3, src_f, all_f, after)
    outputs_ref[0] = output0.astype(BF16)

    scales1 = held_scale1[:, :1]
    total_a1 = sum_end(4, sent_a1, got_a1, hidden_parts[0])
    per_lane = backward_part(held_p1[:, hidden_parts[0]], scales1, total_a1, mix_s1, 0)
    share_start(10, mix_s1, mix_parts[0])
    total_a1 = sum_end(15, sent_a1, got_a1, hidden_parts[1])
    per_lane = per_lane + backward_part(held_p1[:, hidden_parts[1]], scales1, total_a1, mix_s1, 1)
    scale_part(per_lane, scales1, mix_s1)
    share_start(16, mix_s1, mix_parts[1])

    share_wait(10)
    to_table(right_table, 0, 1, mix_s1[:, :cut])
    share_wait(16)
    to_table(right_table, cut // BLK, 1, mix_s1[:, cut:hidden])
    for k in range(capacity):
        block = lax.dot_general(
            left_table[left_index[k]], right_table[right_index[k]],
            (((0,), (0,)), ((), ())), preferred_element_type=F32,
        )
        block_buf[k] = block.astype(BF16)
    for o in range(nd):
        send_buf[o] = block_buf[picks[o]]

    def send_block(k):
        owner = lax.rem(dp + nz + (1 - 2 * (k % 2)) * ((k + 1) // 2), nd)
        remote(
            send_buf.at[owner], recv_buf.at[dp], block_send.at[0], block_recv.at[0],
            (section, owner, tensor),
        ).start()
    loop(0, nd - 1, send_block)
    all_blocks = together(recv_buf.at[: nd - 1], block_send.at[0], block_recv.at[0])
    leaving.append(all_blocks.wait_send)
    coming["blocks", 0] = all_blocks.wait_recv

    both_wait(3)
    product_of(normed_of(flat_rows(all_f), sent_f1), sent_f1)
    sum_start(5, sent_f1, got_f1)

    part_sum = normed_grad_part(mix_s1, 0) + normed_grad_part(mix_s1, 1)
    reduce_start(2, row_grads(part_sum, mix_s1, flat_rows(all_x)), keep_b1, half_b1, other_b1)
    reduce_middle(2, keep_b1, other_b1, chip_b1, rows_b1)

    total_f1 = product_end(5, sent_f1, got_f1)
    mix_f1[mine] = activated_of(*total_f1)
    share_start(11, mix_f1)
    share_wait(11)
    reduce_start(3, jnp.dot(mix_f1[...], down_ref[...], preferred_element_type=F32), keep_f1, half_f1, other_f1)
    reduce_middle(3, keep_f1, other_f1, chip_f1, rows_f1)
    grads_ref[1] = (all_d[core, z].astype(F32) + reduce_end(2, rows_b1)).astype(BF16)
    outputs_ref[1] = (all_f[core, z].astype(F32) + reduce_end(3, rows_f1)).astype(BF16)

    coming.pop(("blocks", 0))()
    for i in range(capacity):
        owned_ref[i] = jnp.where(i < taken, recv_buf[sources[i]].astype(F32), 0.0).astype(BF16)
        filled_ref[i] = jnp.where(i < taken, jnp.ones((1, LANES), F32), 0.0)

    for wait in leaving:
        wait()


def adam(
    outputs_in, grads_in, owned_ref, filled_ref, first_ref, second_ref,
    outputs_ref, grads_ref, first_out, second_out, direction_out,
):
    outputs_ref[...] = outputs_in[...]
    grads_ref[...] = grads_in[...]
    for i in range(owned_ref.shape[0]):
        grad = owned_ref[i].astype(F32)
        filled = filled_ref[i] > 0.5
        first = 0.9 * first_ref[i] + 0.1 * grad
        second = 0.999 * second_ref[i] + 0.001 * grad * grad
        first_out[i] = jnp.where(filled, first, 0.0)
        second_out[i] = jnp.where(filled, second, 0.0)
        direction_out[i] = jnp.where(filled, first / (jnp.sqrt(second) + 1e-08), 0.0)


def by_slot(lists):
    return jnp.transpose(lists, (0, 3, 1, 2))[0]


def body(
    sizes,
    section_inputs, entering, grad_outputs, arriving, live_rows, stashed_inputs, norm_gain,
    up_weight, down_weight, held_blocks, held_count, held_owner, first_moment, second_moment,
):
    ns, nz, nt = sizes
    nd = 2 * nz
    local, width = section_inputs.shape[1:]
    hidden = up_weight.shape[2]
    rows = local * nd
    part = rows // nt
    capacity = held_owner.shape[3]
    turns = stashed_inputs.shape[1]
    blocks = hidden // BLK + width // BLK
    vmem = pl.BlockSpec(memory_space=pltpu.VMEM)
    anywhere = pl.BlockSpec(memory_space=pl.ANY)
    wide = hidden + LANES

    def several(count, shape, dtype):
        return [pltpu.VMEM(shape, dtype) for _ in range(count)]

    scratch = [
        pltpu.VMEM((width, hidden), BF16), pltpu.VMEM((hidden, width), BF16),
        pltpu.SMEM((1,), jnp.int32), pltpu.SMEM((capacity, 1, nd), jnp.int32),
        pltpu.SMEM((nd,), jnp.int32), pltpu.SMEM((capacity, 1, nd), jnp.int32),
        *several(2, (local, width), BF16), pltpu.VMEM((1, width), BF16),
        *several(2, (local, width), BF16),
        pltpu.VMEM((2, nz, 2, local, width), BF16),
        *several(4, (2, nz, local, width), BF16),
        *[pltpu.VMEM((rows, w), BF16) for w in (wide, hidden, wide, wide, hidden, wide)],
        *[pltpu.VMEM((nt, part, w), BF16) for w in (wide, hidden, wide, wide, hidden, wide)],
        *[pltpu.VMEM((rows, w), BF16) for w in (wide, hidden, hidden, hidden, wide, hidden)],
        *several(3, (2, rows // 2, width), F32),
        *several(3, (rows // 2, width), BF16),
        *several(3, (rows // 2, width), BF16),
        *several(3, (nz, local, width), BF16),
        *several(3, (nz, local, width), BF16),
        pltpu.VMEM((2, nz, local, width), BF16), pltpu.VMEM((nd, local, width), BF16),
        *several(2, (blocks, turns * rows, BLK), BF16),
        pltpu.VMEM((capacity, BLK, BLK), BF16),
        *several(2, (nd, BLK, BLK), BF16),
        pltpu.VMEM((part, hidden), F32), pltpu.VMEM((part, LANES), F32),
        pltpu.SemaphoreType.DMA((2,)), pltpu.SemaphoreType.DMA((11,)),
        pltpu.SemaphoreType.DMA((5, 2)), pltpu.SemaphoreType.DMA((5, 2)),
        pltpu.SemaphoreType.DMA((17,)), pltpu.SemaphoreType.DMA((17,)),
        pltpu.SemaphoreType.DMA((4, 2)), pltpu.SemaphoreType.DMA((4, 2)),
        pltpu.SemaphoreType.DMA((1,)), pltpu.SemaphoreType.DMA((1,)),
    ]
    outputs, grads, owned, filled = pl.pallas_call(
        functools.partial(kernel, sizes),
        out_shape=(
            jax.ShapeDtypeStruct((turns, local, width), BF16),
            jax.ShapeDtypeStruct((turns, local, width), BF16),
            jax.ShapeDtypeStruct((capacity, BLK, BLK), BF16),
            jax.ShapeDtypeStruct((capacity, 1, LANES), F32),
        ),
        in_specs=[anywhere] * 12,
        out_specs=[vmem] * 4,
        scratch_shapes=scratch,
        compiler_params=pltpu.CompilerParams(
            collective_id=0, has_side_effects=True, vmem_limit_bytes=56 * 1024 * 1024
        ),
        name="relay",
    )(
        live_rows, by_slot(held_blocks), held_count[0, 0], by_slot(held_owner),
        section_inputs[0], entering[0], grad_outputs[0], arriving[0], stashed_inputs[0], norm_gain,
        up_weight[0], down_weight[0],
    )
    block_shape = jax.ShapeDtypeStruct((capacity, BLK, BLK), F32)
    outputs, grads, first_out, second_out, direction_out = pl.pallas_call(
        adam,
        out_shape=(
            jax.ShapeDtypeStruct(outputs.shape, BF16), jax.ShapeDtypeStruct(grads.shape, BF16),
            block_shape, block_shape, block_shape,
        ),
        in_specs=[vmem] * 6,
        out_specs=[vmem] * 5,
        name="adam",
    )(outputs, grads, owned, filled, first_moment[0, 0, 0], second_moment[0, 0, 0])
    return (
        outputs[None], grads[None],
        first_out[None, None, None], second_out[None, None, None], direction_out[None, None, None],
    )


def solution(mesh):
    sizes = (mesh.shape["section"], mesh.shape["dp"] // 2, mesh.shape["tensor"])
    return jax.shard_map(
        functools.partial(body, sizes),
        mesh=mesh,
        in_specs=(
            P("section", "dp", "tensor"),
            P(None, "dp", "tensor"),
            P("section", "dp", "tensor"),
            P(None, "dp", "tensor"),
            P(),
            P("section", None, "dp", "tensor"),
            P("section", "tensor"),
            P("section", "tensor", "dp"),
            P("section", "dp", "tensor"),
            P("section", "tensor", None, None),
            P("section", "tensor", None),
            P("section", "tensor", None, None),
            P("section", "tensor", "dp", None, None, None),
            P("section", "tensor", "dp", None, None, None),
        ),
        out_specs=(
            P("section", None, "dp", "tensor"),
            P("section", None, "dp", "tensor"),
            P("section", "tensor", "dp", None, None, None),
            P("section", "tensor", "dp", None, None, None),
            P("section", "tensor", "dp", None, None, None),
        ),
        check_vma=False,
    )
```

```python
import functools

import jax
import jax.numpy as jnp
from jax import lax
from jax.experimental import pallas as pl
from jax.experimental.pallas import tpu as pltpu
from jax.sharding import PartitionSpec as P

MESH = pl.DeviceIdType.MESH
BLK = 128
LANES = 128
EPSILON = 1e-06
F32 = jnp.float32
BF16 = jnp.bfloat16


def times_transposed(left, right):
    return lax.dot_general(left, right, (((1,), (1,)), ((), ())), preferred_element_type=F32)


def lane_blocks_sum(value):
    total = value[:, :LANES]
    for start in range(LANES, value.shape[1], LANES):
        total = total + value[:, start : start + LANES]
    return total


def kernel(
    sizes,
    live_hbm, blocks_hbm, count_hbm, owner_hbm,
    section_hbm, entering_hbm, grad_hbm, arriving_hbm, stash_hbm, gain_hbm,
    up_hbm, down_hbm,
    outputs_ref, grads_ref, owned_hbm, filled_hbm,
    up_ref, down_ref,
    live_ref, blocks_ref, count_ref, owner_ref,
    entering_ref, arriving_ref, gain_ref,
    src_f, src_d,
    all_a, all_s, all_x, all_f, all_d,
    sent_p0, sent_a0, sent_f0, sent_p1, sent_a1, sent_f1,
    got_p0, got_a0, got_f0, got_p1, got_a1, got_f1,
    mix_s0, mix_h0, mix_f0, mix_h1, mix_s1, mix_f1,
    keep_f0, keep_b1, keep_f1,
    half_f0, half_b1, half_f1,
    other_f0, other_b1, other_f1,
    chip_f0, chip_b1, chip_f1,
    rows_f0, rows_b1, rows_f1,
    parts_b0, rows_b0,
    left_table, right_table, block_buf, send_buf, recv_buf,
    held_p1, held_scale1, early_blocks, owned_ref, filled_ref, out_sem,
    weight_sem, input_sem,
    gather_send, gather_recv,
    tensor_send, tensor_recv,
    reduce_send, reduce_recv,
    block_send, block_recv,
):
    ns, nz, nt = sizes
    nd = 2 * nz
    local, width = entering_ref.shape
    hidden = up_ref.shape[1]
    rows = local * nd
    part = rows // nt
    dw = width * nt
    section = lax.axis_index("section")
    dp = lax.axis_index("dp")
    tensor = lax.axis_index("tensor")
    z = dp // 2
    core = dp % 2
    partner = (section, z * 2 + 1 - core, tensor)
    after = lax.rem(section + 1, ns)
    before = lax.rem(section + ns - 1, ns)

    leaving = []
    coming = {}

    def remote(src, dst, send_sem, recv_sem, device):
        return pltpu.make_async_remote_copy(
            src_ref=src, dst_ref=dst, send_sem=send_sem, recv_sem=recv_sem,
            device_id=device, device_id_type=MESH,
        )

    def far_first(k):
        return nz // 2 + (1 - 2 * (k % 2)) * ((k + 1) // 2)

    def zup(j):
        return lax.rem(z + j, nz)

    def zdown(j):
        return lax.rem(z + nz - j, nz)

    def tup(j):
        return lax.rem(tensor + j, nt)

    def loop(lo, hi, fn):
        def step(k, carry):
            fn(k)
            return carry
        lax.fori_loop(lo, hi, step, 0)

    weights_up = pltpu.make_async_copy(up_hbm, up_ref, weight_sem.at[0])
    weights_down = pltpu.make_async_copy(down_hbm, down_ref, weight_sem.at[1])

    barrier = pltpu.get_barrier_semaphore()

    def greet(device):
        pl.semaphore_signal(barrier, inc=1, device_id=device, device_id_type=MESH)

    def greet_z(k):
        greet((section, zup(far_first(k)) * 2 + core, tensor))

    loop(0, nz - 1, greet_z)
    greet(partner)
    for j in range(1, nt):
        greet((section, dp, tup(j)))
    greet((after, dp, tensor))
    greet((before, dp, tensor))

    inputs = [
        pltpu.make_async_copy(src, dst, input_sem.at[i])
        for i, (src, dst) in enumerate((
            (stash_hbm.at[0], all_a.at[core, z, 0]), (grad_hbm, all_a.at[core, z, 1]),
            (section_hbm, all_s.at[core, z]), (stash_hbm.at[1], all_x.at[core, z]),
            (entering_hbm, entering_ref), (arriving_hbm, arriving_ref), (gain_hbm, gain_ref),
            (live_hbm, live_ref), (blocks_hbm, blocks_ref), (count_hbm, count_ref), (owner_hbm, owner_ref),
        ))
    ]
    for copy in inputs:
        copy.start()
    weights_up.start()
    weights_down.start()
    for copy in inputs:
        copy.wait()
    recv_buf[dp] = jnp.zeros(recv_buf.shape[1:], BF16)

    pl.semaphore_wait(barrier, nz + (nt - 1) + 2)

    def together(ref, sends, receives):
        return remote(ref, ref, sends, receives, partner)

    def gather_start(g, src, dst, target_section, count):
        def send(k):
            j = far_first(k)
            remote(
                src, dst.at[core, z], gather_send.at[g, 0], gather_recv.at[g, 0],
                (target_section, zup(j) * 2 + core, tensor),
            ).start()
        loop(0, count, send)
        all_of = together(dst.at[0, :count], gather_send.at[g, 0], gather_recv.at[g, 0])
        leaving.append(all_of.wait_send)
        coming["gather", g] = all_of.wait_recv

    def relay(g, dst):
        coming.pop(("gather", g))()
        half = together(dst.at[core], gather_send.at[g, 1], gather_recv.at[g, 1])
        half.start()
        leaving.append(half.wait_send)
        coming["relay", g] = half.wait_recv

    def gather_wait(g):
        coming.pop(("relay", g))()

    def both_start(g, src, dst, target_section):
        def send(k):
            j = far_first(k)
            for other_core in range(2):
                remote(
                    src, dst.at[core, z], gather_send.at[g, 0], gather_recv.at[g, 0],
                    (target_section, zup(j) * 2 + lax.rem(core + other_core, 2), tensor),
                ).start()
        loop(0, nz, send)
        all_of = together(dst, gather_send.at[g, 0], gather_recv.at[g, 0])
        leaving.append(all_of.wait_send)
        coming["both", g] = all_of.wait_recv

    def both_wait(g):
        coming.pop(("both", g))()

    mine = pl.ds(pl.multiple_of(tensor * part, part), part)

    def sum_start(g, sent, got, columns=slice(None)):
        for j in range(1, nt):
            remote(
                sent.at[pl.ds(pl.multiple_of(tup(j) * part, part), part), columns], got.at[j, :, columns],
                tensor_send.at[g], tensor_recv.at[g], (section, dp, tup(j)),
            ).start()
        all_of = together(got.at[1:nt, :, columns], tensor_send.at[g], tensor_recv.at[g])
        leaving.append(all_of.wait_send)
        coming["sum", g] = all_of.wait_recv

    def sum_end(g, sent, got, columns=slice(None)):
        coming.pop(("sum", g))()
        total = sent[mine, columns].astype(F32)
        for j in range(1, nt):
            total = total + got[j, :, columns].astype(F32)
        return total

    def share_start(g, mix, columns=slice(None)):
        for j in range(1, nt):
            remote(
                mix.at[mine, columns], mix.at[mine, columns],
                tensor_send.at[g], tensor_recv.at[g], (section, dp, tup(j)),
            ).start()
        all_of = together(mix.at[: (nt - 1) * part, columns], tensor_send.at[g], tensor_recv.at[g])
        leaving.append(all_of.wait_send)
        coming["share", g] = all_of.wait_recv

    def share_wait(g):
        coming.pop(("share", g))()

    def reduce_start(g, value, keep, half, other):
        keep[...] = value.reshape(2, rows // 2, width)
        half[...] = keep[1 - core].astype(BF16)
        swap = remote(half, other, reduce_send.at[g, 0], reduce_recv.at[g, 0], partner)
        swap.start()
        leaving.append(swap.wait_send)
        coming["swap", g] = swap.wait_recv

    def reduce_middle(g, keep, other, chip, got):
        coming.pop(("swap", g))()
        total = keep[core] + other[...].astype(F32)
        chip[...] = total.reshape(nz, local, width).astype(BF16)
        got[z] = chip[z]

        def send(k):
            j = far_first(k)
            remote(
                chip.at[zup(j)], got.at[z], reduce_send.at[g, 1], reduce_recv.at[g, 1],
                (section, zup(j) * 2 + core, tensor),
            ).start()
        loop(0, nz - 1, send)
        all_of = together(got.at[: nz - 1], reduce_send.at[g, 1], reduce_recv.at[g, 1])
        leaving.append(all_of.wait_send)
        coming["reduce", g] = all_of.wait_recv

    def reduce_end(g, got):
        coming.pop(("reduce", g))()
        return jnp.sum(got[...].astype(F32), axis=0)

    def scatter_start(g, value, parts, got):
        parts[...] = value.reshape(parts.shape).astype(BF16)
        got[dp] = parts[core, z]

        def send(j, other_core):
            target = lax.rem(core + other_core, 2)
            remote(
                parts.at[target, zup(j)], got.at[dp], reduce_send.at[g, 0], reduce_recv.at[g, 0],
                (section, zup(j) * 2 + target, tensor),
            ).start()

        def send_both(k):
            send(far_first(k), 0)
            send(far_first(k), 1)
        loop(0, nz - 1, send_both)
        send(0, 1)
        all_of = together(got.at[: nd - 1], reduce_send.at[g, 0], reduce_recv.at[g, 0])
        leaving.append(all_of.wait_send)
        coming["scatter", g] = all_of.wait_recv

    def scatter_end(g, got):
        coming.pop(("scatter", g))()
        return jnp.sum(got[...].astype(F32), axis=0)

    def flat_rows(ref):
        return ref[...].astype(F32).reshape(rows, width)

    gain = gain_ref[...].astype(F32)

    def scales_of(lane_squares):
        return lax.rsqrt(jnp.sum(lane_squares, axis=1, keepdims=True) / dw + EPSILON)

    cut = hidden // LANES // 2 * LANES
    hidden_parts = (slice(0, cut), slice(cut, hidden))
    product_parts = (slice(0, LANES + cut), slice(LANES + cut, LANES + hidden))
    mix_parts = (slice(0, cut), slice(cut, hidden + LANES))

    def normed_of(widened, sent):
        sent[:, :LANES] = lane_blocks_sum(widened * widened).astype(BF16)
        return (widened * gain).astype(BF16)

    def product_of(normed, sent):
        sent[:, LANES:] = jnp.dot(normed, up_ref[...], preferred_element_type=F32).astype(BF16)

    def product_part(normed, sent, i):
        columns = hidden_parts[i]
        product = jnp.dot(normed, up_ref[:, columns], preferred_element_type=F32)
        sent[:, LANES + columns.start : LANES + columns.stop] = product.astype(BF16)

    def act_grad_part(grads, sent, i):
        columns = hidden_parts[i]
        sent[:, columns] = times_transposed(grads, down_ref[columns, :]).astype(BF16)

    def to_table(table, first, turn, value):
        for b in range(value.shape[1] // BLK):
            table[first + b, turn * rows : (turn + 1) * rows, :] = value[:, b * BLK : (b + 1) * BLK]

    hidden_blocks = hidden // BLK
    channel_blocks = width // BLK

    def backward_part(product, scales, act_grad, mix, i):
        inner = product * scales
        gate = jax.nn.sigmoid(inner)
        hidden_grad = act_grad * gate * (1.0 + inner * (1.0 - gate))
        mix[mine, hidden_parts[i]] = (hidden_grad * scales).astype(BF16)
        return lane_blocks_sum(hidden_grad * product)

    def scale_part(per_lane, scales, mix):
        mix[mine, hidden:] = (per_lane * (scales * scales * scales / dw)).astype(BF16)

    def block_of(k, turn_rows):
        return lax.dot_general(
            left_table[left_index[k], turn_rows], right_table[right_index[k], turn_rows],
            (((0,), (0,)), ((), ())), preferred_element_type=F32,
        )

    def activated_of(product, scales):
        inner = product * scales
        return (inner * jax.nn.sigmoid(inner)).astype(BF16)

    def product_end(g, sent, got):
        total = sum_end(g, sent, got)
        return total[:, LANES:], scales_of(total[:, :LANES])

    def normed_grad_part(mix, i):
        columns = hidden_parts[i]
        return times_transposed(mix[:, columns], up_ref[:, columns])

    def row_grads(part_sum, mix, widened):
        coefficient = jnp.sum(mix[:, hidden:].astype(F32), axis=1, keepdims=True)
        return part_sum * gain - coefficient * widened

    def rows_of(ref, which):
        return ref[:, :, which].astype(F32).reshape(rows, width)

    gather_start(0, all_a.at[core, z], all_a, section, nz - 1)
    capacity = owner_ref.shape[0]
    up_count = hidden_blocks * channel_blocks
    left_index, right_index = [], []
    for k in range(capacity):
        number = blocks_ref[k, 0, dp]
        down_number = jnp.maximum(number - up_count, 0)
        is_up = number < up_count
        left_index.append(
            jnp.where(is_up, number // hidden_blocks, channel_blocks + down_number // channel_blocks)
        )
        right_index.append(
            jnp.where(is_up, number % hidden_blocks, hidden_blocks + down_number % channel_blocks)
        )
    my_count = count_ref[dp]
    my_owners = [owner_ref[k, 0, dp] for k in range(capacity)]
    picks = []
    for o in range(nd):
        pick = jnp.int32(0)
        for k in range(capacity):
            pick = jnp.where((my_owners[k] == o) & (k < my_count), k, pick)
        picks.append(pick)
    taken = jnp.int32(0)
    sources = [jnp.int32(0) for _ in range(capacity)]
    for h in range(nd):
        sends = jnp.int32(0)
        for k in range(capacity):
            sends = jnp.where((owner_ref[k, 0, h] == dp) & (k < count_ref[h]), 1, sends)
        for i in range(capacity):
            sources[i] = jnp.where((sends == 1) & (taken == i), h, sources[i])
        taken = taken + sends

    relay(0, all_a)
    gather_start(1, all_s.at[core, z], all_s, section, nz - 1)
    gather_start(4, all_x.at[core, z], all_x, section, nz - 1)
    weights_up.wait()
    gather_wait(0)
    normed0 = normed_of(rows_of(all_a, 0), sent_p0)
    product_part(normed0, sent_p0, 0)
    sum_start(0, sent_p0, got_p0, product_parts[0])
    weights_down.wait()
    dy0 = rows_of(all_a, 1).astype(BF16)
    act_grad_part(dy0, sent_a0, 0)
    sum_start(1, sent_a0, got_a0, hidden_parts[0])
    product_part(normed0, sent_p0, 1)
    sum_start(12, sent_p0, got_p0, product_parts[1])
    act_grad_part(dy0, sent_a0, 1)
    sum_start(13, sent_a0, got_a0, hidden_parts[1])
    to_table(left_table, 0, 0, normed0)
    to_table(right_table, hidden_blocks, 0, dy0)

    relay(1, all_s)
    gather_wait(1)
    product_of(normed_of(flat_rows(all_s), sent_f0), sent_f0)

    total_p0 = sum_end(0, sent_p0, got_p0, product_parts[0])
    scales0 = scales_of(total_p0[:, :LANES])
    first_p0 = total_p0[:, LANES:]
    total_a0 = sum_end(1, sent_a0, got_a0, hidden_parts[0])
    per_lane = backward_part(first_p0, scales0, total_a0, mix_s0, 0)
    share_start(6, mix_s0, mix_parts[0])
    last_p0 = sum_end(12, sent_p0, got_p0, product_parts[1])
    total_a0 = sum_end(13, sent_a0, got_a0, hidden_parts[1])
    scale_part(per_lane + backward_part(last_p0, scales0, total_a0, mix_s0, 1), scales0, mix_s0)
    share_start(14, mix_s0, mix_parts[1])
    sum_start(2, sent_f0, got_f0)
    mix_h0[mine, hidden_parts[0]] = activated_of(first_p0, scales0)
    mix_h0[mine, hidden_parts[1]] = activated_of(last_p0, scales0)

    relay(4, all_x)
    gather_wait(4)
    normed1 = normed_of(flat_rows(all_x), sent_p1)
    product_of(normed1, sent_p1)
    to_table(left_table, 0, 1, normed1)

    share_wait(6)
    part_sum = normed_grad_part(mix_s0, 0)
    share_wait(14)
    part_sum = part_sum + normed_grad_part(mix_s0, 1)
    scatter_start(0, row_grads(part_sum, mix_s0, rows_of(all_a, 0)), parts_b0, rows_b0)
    sum_start(3, sent_p1, got_p1)
    to_table(right_table, 0, 0, mix_s0[:, :hidden])
    total_f0 = product_end(2, sent_f0, got_f0)
    mix_f0[mine] = activated_of(*total_f0)
    share_start(7, mix_f0)
    share_start(8, mix_h0)

    row_ids = dp * local + lax.broadcasted_iota(jnp.int32, (local, width), 0)
    masked = jnp.where(row_ids < live_ref[0, 0, 0], arriving_ref[...].astype(F32), 0.0)
    input_grad0 = all_a[core, z, 1].astype(F32) + scatter_end(0, rows_b0)
    src_d[...] = jnp.where(section == 0, masked, input_grad0).astype(BF16)
    both_start(2, src_d, all_d, before)
    grads_ref[0] = input_grad0.astype(BF16)

    total_p1, scales1 = product_end(3, sent_p1, got_p1)
    held_p1[...] = total_p1
    held_scale1[...] = jnp.broadcast_to(scales1, held_scale1.shape)
    mix_h1[mine] = activated_of(total_p1, scales1)
    share_start(9, mix_h1)
    share_wait(7)
    reduce_start(1, jnp.dot(mix_f0[...], down_ref[...], preferred_element_type=F32), keep_f0, half_f0, other_f0)
    reduce_middle(1, keep_f0, other_f0, chip_f0, rows_f0)
    share_wait(8)
    to_table(left_table, channel_blocks, 0, mix_h0[...])

    both_wait(2)
    dy1 = flat_rows(all_d).astype(BF16)
    act_grad_part(dy1, sent_a1, 0)
    sum_start(4, sent_a1, got_a1, hidden_parts[0])
    act_grad_part(dy1, sent_a1, 1)
    sum_start(15, sent_a1, got_a1, hidden_parts[1])
    to_table(right_table, hidden_blocks, 1, dy1)
    share_wait(9)
    to_table(left_table, channel_blocks, 1, mix_h1[...])

    output0 = all_s[core, z].astype(F32) + reduce_end(1, rows_f0)
    src_f[...] = jnp.where(section == ns - 1, entering_ref[...].astype(F32), output0).astype(BF16)
    both_start(3, src_f, all_f, after)
    outputs_ref[0] = output0.astype(BF16)

    scales1 = held_scale1[:, :1]
    total_a1 = sum_end(4, sent_a1, got_a1, hidden_parts[0])
    per_lane = backward_part(held_p1[:, hidden_parts[0]], scales1, total_a1, mix_s1, 0)
    share_start(10, mix_s1, mix_parts[0])
    total_a1 = sum_end(15, sent_a1, got_a1, hidden_parts[1])
    per_lane = per_lane + backward_part(held_p1[:, hidden_parts[1]], scales1, total_a1, mix_s1, 1)
    scale_part(per_lane, scales1, mix_s1)
    share_start(16, mix_s1, mix_parts[1])

    for k in range(capacity):
        early_blocks[k] = block_of(k, slice(0, rows))
    share_wait(10)
    to_table(right_table, 0, 1, mix_s1[:, :cut])
    share_wait(16)
    to_table(right_table, cut // BLK, 1, mix_s1[:, cut:hidden])
    for k in range(capacity):
        block_buf[k] = (early_blocks[k] + block_of(k, slice(rows, 2 * rows))).astype(BF16)
    for o in range(nd):
        send_buf[o] = block_buf[picks[o]]

    def send_block(k):
        owner = lax.rem(dp + nz + (1 - 2 * (k % 2)) * ((k + 1) // 2), nd)
        remote(
            send_buf.at[owner], recv_buf.at[dp], block_send.at[0], block_recv.at[0],
            (section, owner, tensor),
        ).start()
    loop(0, nd - 1, send_block)
    all_blocks = together(recv_buf.at[: nd - 1], block_send.at[0], block_recv.at[0])
    leaving.append(all_blocks.wait_send)
    coming["blocks", 0] = all_blocks.wait_recv

    both_wait(3)
    product_of(normed_of(flat_rows(all_f), sent_f1), sent_f1)
    sum_start(5, sent_f1, got_f1)

    part_sum = normed_grad_part(mix_s1, 0) + normed_grad_part(mix_s1, 1)
    reduce_start(2, row_grads(part_sum, mix_s1, flat_rows(all_x)), keep_b1, half_b1, other_b1)
    reduce_middle(2, keep_b1, other_b1, chip_b1, rows_b1)

    total_f1 = product_end(5, sent_f1, got_f1)
    mix_f1[mine] = activated_of(*total_f1)
    share_start(11, mix_f1)
    share_wait(11)
    reduce_start(3, jnp.dot(mix_f1[...], down_ref[...], preferred_element_type=F32), keep_f1, half_f1, other_f1)
    reduce_middle(3, keep_f1, other_f1, chip_f1, rows_f1)
    coming.pop(("blocks", 0))()
    for i in range(capacity):
        owned_ref[i] = jnp.where(i < taken, recv_buf[sources[i]].astype(F32), 0.0).astype(BF16)
        filled_ref[i] = jnp.where(i < taken, jnp.ones((1, LANES), F32), 0.0)
    blocks_out = (
        pltpu.make_async_copy(owned_ref, owned_hbm, out_sem.at[0]),
        pltpu.make_async_copy(filled_ref, filled_hbm, out_sem.at[1]),
    )
    for copy in blocks_out:
        copy.start()
    grads_ref[1] = (all_d[core, z].astype(F32) + reduce_end(2, rows_b1)).astype(BF16)
    outputs_ref[1] = (all_f[core, z].astype(F32) + reduce_end(3, rows_f1)).astype(BF16)
    for copy in blocks_out:
        copy.wait()

    for wait in leaving:
        wait()


def adam(
    outputs_in, grads_in, owned_ref, filled_ref, first_ref, second_ref,
    outputs_ref, grads_ref, first_out, second_out, direction_out,
):
    outputs_ref[...] = outputs_in[...]
    grads_ref[...] = grads_in[...]
    for i in range(owned_ref.shape[0]):
        grad = owned_ref[i].astype(F32)
        filled = filled_ref[i] > 0.5
        first = 0.9 * first_ref[i] + 0.1 * grad
        second = 0.999 * second_ref[i] + 0.001 * grad * grad
        first_out[i] = jnp.where(filled, first, 0.0)
        second_out[i] = jnp.where(filled, second, 0.0)
        direction_out[i] = jnp.where(filled, first / (jnp.sqrt(second) + 1e-08), 0.0)


def by_slot(lists):
    return jnp.transpose(lists, (0, 3, 1, 2))[0]


def body(
    sizes,
    section_inputs, entering, grad_outputs, arriving, live_rows, stashed_inputs, norm_gain,
    up_weight, down_weight, held_blocks, held_count, held_owner, first_moment, second_moment,
):
    ns, nz, nt = sizes
    nd = 2 * nz
    local, width = section_inputs.shape[1:]
    hidden = up_weight.shape[2]
    rows = local * nd
    part = rows // nt
    capacity = held_owner.shape[3]
    turns = stashed_inputs.shape[1]
    blocks = hidden // BLK + width // BLK
    vmem = pl.BlockSpec(memory_space=pltpu.VMEM)
    anywhere = pl.BlockSpec(memory_space=pl.ANY)
    wide = hidden + LANES

    def several(count, shape, dtype):
        return [pltpu.VMEM(shape, dtype) for _ in range(count)]

    scratch = [
        pltpu.VMEM((width, hidden), BF16), pltpu.VMEM((hidden, width), BF16),
        pltpu.SMEM((1, 1, 1), jnp.int32), pltpu.SMEM((capacity, 1, nd), jnp.int32),
        pltpu.SMEM((nd,), jnp.int32), pltpu.SMEM((capacity, 1, nd), jnp.int32),
        *several(2, (local, width), BF16), pltpu.VMEM((1, width), BF16),
        *several(2, (local, width), BF16),
        pltpu.VMEM((2, nz, 2, local, width), BF16),
        *several(4, (2, nz, local, width), BF16),
        *[pltpu.VMEM((rows, w), BF16) for w in (wide, hidden, wide, wide, hidden, wide)],
        *[pltpu.VMEM((nt, part, w), BF16) for w in (wide, hidden, wide, wide, hidden, wide)],
        *[pltpu.VMEM((rows, w), BF16) for w in (wide, hidden, hidden, hidden, wide, hidden)],
        *several(3, (2, rows // 2, width), F32),
        *several(3, (rows // 2, width), BF16),
        *several(3, (rows // 2, width), BF16),
        *several(3, (nz, local, width), BF16),
        *several(3, (nz, local, width), BF16),
        pltpu.VMEM((2, nz, local, width), BF16), pltpu.VMEM((nd, local, width), BF16),
        *several(2, (blocks, turns * rows, BLK), BF16),
        pltpu.VMEM((capacity, BLK, BLK), BF16),
        *several(2, (nd, BLK, BLK), BF16),
        pltpu.VMEM((part, hidden), F32), pltpu.VMEM((part, LANES), F32),
        pltpu.VMEM((capacity, BLK, BLK), F32),
        pltpu.VMEM((capacity, BLK, BLK), BF16), pltpu.VMEM((capacity, 1, LANES), F32),
        pltpu.SemaphoreType.DMA((2,)),
        pltpu.SemaphoreType.DMA((2,)), pltpu.SemaphoreType.DMA((11,)),
        pltpu.SemaphoreType.DMA((5, 2)), pltpu.SemaphoreType.DMA((5, 2)),
        pltpu.SemaphoreType.DMA((17,)), pltpu.SemaphoreType.DMA((17,)),
        pltpu.SemaphoreType.DMA((4, 2)), pltpu.SemaphoreType.DMA((4, 2)),
        pltpu.SemaphoreType.DMA((1,)), pltpu.SemaphoreType.DMA((1,)),
    ]
    outputs, grads, owned, filled = pl.pallas_call(
        functools.partial(kernel, sizes),
        out_shape=(
            jax.ShapeDtypeStruct((turns, local, width), BF16),
            jax.ShapeDtypeStruct((turns, local, width), BF16),
            jax.ShapeDtypeStruct((capacity, BLK, BLK), BF16),
            jax.ShapeDtypeStruct((capacity, 1, LANES), F32),
        ),
        in_specs=[anywhere] * 12,
        out_specs=[vmem] * 2 + [anywhere] * 2,
        scratch_shapes=scratch,
        compiler_params=pltpu.CompilerParams(
            collective_id=0, has_side_effects=True, vmem_limit_bytes=56 * 1024 * 1024
        ),
        name="relay",
    )(
        live_rows.reshape(1, 1, 1), by_slot(held_blocks), held_count[0, 0], by_slot(held_owner),
        section_inputs[0], entering[0], grad_outputs[0], arriving[0], stashed_inputs[0], norm_gain,
        up_weight[0], down_weight[0],
    )
    block_shape = jax.ShapeDtypeStruct((capacity, BLK, BLK), F32)
    outputs, grads, first_out, second_out, direction_out = pl.pallas_call(
        adam,
        out_shape=(
            jax.ShapeDtypeStruct(outputs.shape, BF16), jax.ShapeDtypeStruct(grads.shape, BF16),
            block_shape, block_shape, block_shape,
        ),
        in_specs=[vmem] * 6,
        out_specs=[vmem] * 5,
        name="adam",
    )(outputs, grads, owned, filled, first_moment[0, 0, 0], second_moment[0, 0, 0])
    return (
        outputs[None], grads[None],
        first_out[None, None, None], second_out[None, None, None], direction_out[None, None, None],
    )


def solution(mesh):
    sizes = (mesh.shape["section"], mesh.shape["dp"] // 2, mesh.shape["tensor"])
    return jax.shard_map(
        functools.partial(body, sizes),
        mesh=mesh,
        in_specs=(
            P("section", "dp", "tensor"),
            P(None, "dp", "tensor"),
            P("section", "dp", "tensor"),
            P(None, "dp", "tensor"),
            P(),
            P("section", None, "dp", "tensor"),
            P("section", "tensor"),
            P("section", "tensor", "dp"),
            P("section", "dp", "tensor"),
            P("section", "tensor", None, None),
            P("section", "tensor", None),
            P("section", "tensor", None, None),
            P("section", "tensor", "dp", None, None, None),
            P("section", "tensor", "dp", None, None, None),
        ),
        out_specs=(
            P("section", None, "dp", "tensor"),
            P("section", None, "dp", "tensor"),
            P("section", "tensor", "dp", None, None, None),
            P("section", "tensor", "dp", None, None, None),
            P("section", "tensor", "dp", None, None, None),
        ),
        check_vma=False,
    )
```
